256 devices in a mesh: space: 128 (over y, z, x), mp: 2 (over core).
Axes of the slice: x: 4, y: 4, z: 8, core: 2. Of those that a mesh axis runs over, the one named last changes fastest.
Arguments:
- points: bfloat16 [262144, 512], P('space'), may hold values from -40 to 40
- curve_rank: int32 [262144], P('space'), may hold values from 0 to 262143, as said below
- patch_counts: int32 [128, 4], P('space'), may hold values from 1 to 1024, 2048 in all within a row
- norm_gain_attn: float32 [512], replicated, may hold values from 0.1 to 1.9
- w_qkv: bfloat16 [3, 512, 512], P(None, None, 'mp'), may hold values from -1.5 to 1.5
- w_out: bfloat16 [512, 512], P('mp'), may hold values from -0.75 to 0.75
- norm_gain_mlp: float32 [512], replicated, may hold values from 0.1 to 1.9
- w_fc1: bfloat16 [512, 2048], P(None, 'mp'), may hold values from -0.25 to 0.25
- w_fc2: bfloat16 [2048, 512], P('mp'), may hold values from -0.1875 to 0.1875
Outputs:
- layer_out: bfloat16 [262144, 512], P('space')
The draws below stay inside these ranges and needn't reach their ends.
Inputs may be any that keep to these rules, and one draw needn't show every extreme that they name: curve_rank is a permutation; the points of shard a take exactly the positions b * 2048 + a * 16 + m for every owner b and every m below 16. `patch_counts`: each row sums to 2048.
All inputs are finite; a program needn't handle non-finite values.
Results may differ from the reference program's by a relative error of at most 0.0075.
Values may be sent and summed in bfloat16 or wider, within the bound.
A program may use at most 128 MiB of HBM per device.

```python
import math
import jax
import jax.numpy as jnp
import numpy as np
from jax import lax

D = 512
FF = 2048
PATCH = 1024
P_DEV = 2048
HDIM = 64
TILES = 4
SHARDS = 128
CELL = 16
NPTS = 262144


def draw_points(key, part):
    subkeys = jax.random.split(jax.random.fold_in(key, 11), 4)
    normal_part = jax.random.normal(subkeys[0], (NPTS, D), jnp.float32)
    row_scale = jnp.exp(jax.random.uniform(subkeys[1], (NPTS, 1), jnp.float32, math.log(0.5), math.log(2.0)))
    column_scale = jnp.exp(jax.random.uniform(subkeys[2], (1, D), jnp.float32, math.log(0.4), math.log(4.0)))
    offset = 0.5 * jax.random.normal(subkeys[3], (NPTS, 1), jnp.float32)
    values = (normal_part * column_scale + offset) * row_scale
    return jnp.clip(values, -40.0, 40.0).astype(jnp.bfloat16)


def draw_w_qkv(key, part):
    subkeys = jax.random.split(jax.random.fold_in(key, 23), 1)
    normal_part = jax.random.normal(subkeys[0], (3, D, D), jnp.float32) / math.sqrt(D)
    factor = jnp.array([1.4142, 1.4142, 1.0], jnp.float32)[:, None, None]
    weights = normal_part * factor
    return jnp.clip(weights, -1.5, 1.5).astype(jnp.bfloat16)


def draw_curve_rank(key, part):
    subkeys = jax.random.split(jax.random.fold_in(key, 5), SHARDS)

    def per_shard(shard_key):
        return jax.random.permutation(shard_key, P_DEV)
    local_slot = jax.vmap(per_shard)(subkeys).astype(jnp.int32)
    device = jnp.arange(SHARDS, dtype=jnp.int32)[:, None]
    positions = local_slot // CELL * P_DEV + device * CELL + local_slot % CELL
    return positions.reshape(NPTS).astype(jnp.int32)


def level_of(rng, dims, cuts, low, largest):
    level, own = 1.0, jax.random.fold_in(rng, 6)
    for axis_at, blocks in cuts:
        heights = jnp.exp(jax.random.uniform(jax.random.fold_in(own, axis_at), (blocks,), jnp.float32, low / len(cuts), largest / len(cuts)))
        level = level * jnp.repeat(heights, dims[axis_at] // blocks).reshape([-1 if axis == axis_at else 1 for axis in range(len(dims))])
    return level


def length_profile(amount, total, limit, lean):
    weights = [(1 << 20) // math.isqrt(rank ** lean) + 1 for rank in range(2, amount + 1)]
    spare, holding = total - limit - (amount - 1), [1] * (amount - 1)
    while spare > 0:
        free = [i for i in range(amount - 1) if holding[i] < limit]
        pool, budget = sum([weights[i] for i in free]), spare
        for i in free:
            more = min(limit - holding[i], max(1, budget * weights[i] // pool), spare)
            holding[i] = holding[i] + more
            spare = spare - more
    return np.array([limit] + holding)


def uneven(stream_key, amount, total, reach, skew):
    if amount == 2:
        one = jax.random.randint(stream_key, (), max(1, total - reach), min(reach, total - 1) + 1)
        return jnp.stack([one, total - one])
    lengths = jnp.asarray(length_profile(amount, total, reach, skew), jnp.int32)
    couples = (amount - 1) // 2
    donor, taker = lengths[1:1 + 2 * couples:2], lengths[2:2 + 2 * couples:2]
    slack = jnp.minimum(donor - 1, reach - taker)
    moved = jax.random.randint(jax.random.fold_in(stream_key, 1), (couples,), 0, 1 << 20) % (slack + 1)
    lengths = lengths.at[1:1 + 2 * couples:2].set(donor - moved).at[2:2 + 2 * couples:2].set(taker + moved)
    return lengths[jax.random.permutation(jax.random.fold_in(stream_key, 2), amount)]


def bell_draw(key, shape, deviation, most, cuts=(), kind=jnp.bfloat16):
    level = level_of(key, shape, cuts, -0.22, 0.18) if cuts else 1.0
    values = jax.random.normal(key, shape, jnp.float32) * deviation * level
    return jnp.minimum(jnp.maximum(values, -most), most).astype(kind)


def setup_inputs(seed: int = 0) -> dict:
    keys = jax.random.split(jax.random.key(seed), 10)
    return {
        "points": draw_points(jax.random.fold_in(keys[9], 71), 0),
        "curve_rank": draw_curve_rank(jax.random.fold_in(keys[9], 71), 0),
        "patch_counts": jax.vmap(lambda own: uneven(own, TILES, P_DEV, PATCH, 2))(jax.random.split(keys[2], SHARDS)).reshape((SHARDS, TILES)).astype(jnp.int32),
        "norm_gain_attn": jnp.clip(1.0 + 0.18 * jax.random.normal(keys[3], (D,), jnp.float32), 0.1, 1.9),
        "w_qkv": draw_w_qkv(jax.random.fold_in(keys[9], 71), 0),
        "w_out": bell_draw(keys[5], (D, D), (D // 8) ** -0.5, 0.75, ((0, 2),)),
        "norm_gain_mlp": jnp.clip(1.0 + 0.18 * jax.random.normal(keys[6], (D,), jnp.float32), 0.1, 1.9),
        "w_fc1": bell_draw(keys[7], (D, FF), D ** -0.5, 0.25, ((1, 2),)),
        "w_fc2": bell_draw(keys[8], (FF, D), (FF // 2) ** -0.5, 0.1875, ((0, 2),)),
    }


epsilon = 1e-06

def layer_norm(inputs, gain_row):
    values = inputs.astype(jnp.float32)
    average = lax.optimization_barrier(jnp.mean(values, axis=-1, keepdims=True))
    centred = values - average
    second = lax.optimization_barrier(jnp.mean(centred * centred, axis=-1, keepdims=True))
    return (centred * lax.rsqrt(second + epsilon) * gain_row).astype(jnp.bfloat16)

def tile_layout(counts, tile_width):
    starts = (jnp.cumsum(counts) - counts).astype(jnp.int32)
    offsets = jnp.arange(tile_width, dtype=jnp.int32)
    usable = offsets[None, :] < counts[:, None]
    source = jnp.where(usable, starts[:, None] + offsets[None, :], 0).astype(jnp.int32)
    return (starts, source, usable)

def back_index(starts, length, tile_width):
    places = jnp.arange(length, dtype=jnp.int32)
    covered = starts[None, :] <= places[:, None]
    owning = lax.optimization_barrier(jnp.sum(covered.astype(jnp.int32), axis=1)) - 1
    start_of = lax.optimization_barrier(jnp.max(jnp.where(covered, starts[None, :], 0), axis=1))
    return (owning * tile_width + places - start_of).astype(jnp.int32)

def attend(queries, key_rows, value_rows, counts):
    length, columns = queries.shape
    head_count = columns // HDIM
    score_scale = 1.0 / math.sqrt(HDIM)
    starts, source, usable = tile_layout(counts, PATCH)

    def one_tile(packed):
        picked, allowed = packed
        tile_q = queries[picked].reshape(PATCH, head_count, HDIM).astype(jnp.float32)
        tile_k = key_rows[picked].reshape(PATCH, head_count, HDIM).astype(jnp.float32)
        tile_v = value_rows[picked].reshape(PATCH, head_count, HDIM).astype(jnp.float32)
        scores = jnp.einsum('qhd,khd->hqk', tile_q, tile_k) * score_scale
        scores = jnp.where(allowed[None, None, :], scores, -jnp.inf)
        highest = lax.optimization_barrier(jnp.max(scores, axis=2, keepdims=True))
        raised = jnp.exp(scores - highest)
        weights = (raised / lax.optimization_barrier(jnp.sum(raised, axis=2, keepdims=True))).astype(jnp.bfloat16)
        context = jnp.einsum('hqk,khd->qhd', weights.astype(jnp.float32), tile_v)
        return context.astype(jnp.bfloat16).reshape(PATCH, columns)
    tile_out = lax.map(one_tile, (source, usable))
    places = back_index(starts, length, PATCH)
    return tile_out.reshape(-1, columns)[places]

def reference(points, curve_rank, patch_counts, norm_gain_attn, w_qkv, w_out, norm_gain_mlp, w_fc1, w_fc2):
    normed = layer_norm(points, norm_gain_attn)
    ordered = jnp.zeros_like(normed).at[curve_rank].set(normed)
    owner_blocks = ordered.reshape(SHARDS, P_DEV, D)

    def owner_step(packed):
        owner_rows, counts = packed
        queries = jnp.dot(owner_rows, w_qkv[0], preferred_element_type=jnp.float32).astype(jnp.bfloat16)
        key_rows = jnp.dot(owner_rows, w_qkv[1], preferred_element_type=jnp.float32).astype(jnp.bfloat16)
        value_rows = jnp.dot(owner_rows, w_qkv[2], preferred_element_type=jnp.float32).astype(jnp.bfloat16)
        return attend(queries, key_rows, value_rows, counts)
    context = lax.map(owner_step, (owner_blocks, patch_counts)).reshape(NPTS, D)
    gathered = context[curve_rank]

    def finish(packed):
        rows_ctx, rows_in = packed
        attn_out = jnp.dot(rows_ctx, w_out, preferred_element_type=jnp.float32).astype(jnp.bfloat16)
        middle = (rows_in.astype(jnp.float32) + attn_out.astype(jnp.float32)).astype(jnp.bfloat16)
        normed_mlp = layer_norm(middle, norm_gain_mlp)
        hidden = jax.nn.gelu(jnp.dot(normed_mlp, w_fc1, preferred_element_type=jnp.float32), approximate=True).astype(jnp.bfloat16)
        return (middle.astype(jnp.float32) + jnp.dot(hidden, w_fc2, preferred_element_type=jnp.float32)).astype(jnp.bfloat16)
    finished = lax.map(finish, (gathered.reshape(SHARDS, P_DEV, D), points.reshape(SHARDS, P_DEV, D)))
    return finished.reshape(NPTS, D)
```

```python
import functools
import math

import jax
import jax.numpy as jnp
from jax import lax
from jax.experimental import pallas as pl
from jax.experimental.pallas import tpu as pltpu
from jax.sharding import PartitionSpec as P

HDIM = 64
EPS = 1e-06
FAR = -1e30
QSCALE = math.log2(math.e) / math.sqrt(HDIM)

LENGTH = 2048
FEAT = 512
HALF = 1024
SHARDS = 128
PEERS = 64
CELL = 16
GROUP = 256
GROUPS = 4
NX, NZ = 4, 8

MESH = pl.DeviceIdType.MESH
VMEM = pltpu.VMEM
F32 = jnp.float32
BF16 = jnp.bfloat16


def dot(a, b):
    return jnp.dot(a, b, preferred_element_type=F32)


def norm_rows(values, gain):
    average = jnp.mean(values, axis=-1, keepdims=True)
    centred = values - average
    second = jnp.mean(centred * centred, axis=-1, keepdims=True)
    return (centred * lax.rsqrt(second + EPS) * gain).astype(BF16)


class Place:
    def __init__(self):
        self.s = lax.axis_index("space")
        self.c = lax.axis_index("mp")
        self.x = lax.rem(self.s, NX)
        self.z = lax.rem(self.s // NX, NZ)
        self.h = self.s // PEERS
        self.own = self.s - self.h * PEERS
        self.partner = (self.s, 1 - self.c)
        self.has_self = self.h == self.c

    def group(self, j):
        near = self.z // (NZ // 2)
        zh = (1 - near) if j < 2 else near
        return (j % 2) * 2 + zh

    def peer(self, group, q):
        zz = lax.rem(q // NX + self.z, NZ // 2)
        xx = lax.rem(q + self.x, NX)
        return group * 16 + zz * NX + xx


def greet(me):
    barrier = pltpu.get_barrier_semaphore()

    def one(i, carry):
        peer = lax.rem(me.own + i, PEERS)

        @pl.when(jnp.logical_not(me.has_self & (i == 0)))
        def _():
            pl.semaphore_signal(
                barrier, inc=1, device_id=(me.c * PEERS + peer, me.h), device_id_type=MESH
            )

        return carry

    lax.fori_loop(0, PEERS, one, 0)
    pl.semaphore_signal(barrier, inc=1, device_id=me.partner, device_id_type=MESH)
    return barrier


def await_greetings(me, barrier):
    pl.semaphore_wait(barrier, jnp.where(me.has_self, PEERS, PEERS + 1))


def send_group(me, group, src, dst, send_sem, recv_sem):
    landing = pl.multiple_of(me.s * CELL, CELL)
    mine = me.own // 16

    def one(q, carry):
        peer = me.peer(group, q)
        rows = pl.ds(pl.multiple_of(peer * CELL, CELL), CELL)
        itself = me.has_self & (peer == me.own)

        @pl.when(itself)
        def _():
            pltpu.make_async_copy(
                src.at[rows], dst.at[pl.ds(landing, CELL)], recv_sem.at[mine]
            ).start()

        @pl.when(jnp.logical_not(itself))
        def _():
            pltpu.make_async_remote_copy(
                src_ref=src.at[rows],
                dst_ref=dst.at[pl.ds(landing, CELL)],
                send_sem=send_sem,
                recv_sem=recv_sem.at[mine],
                device_id=(me.c * PEERS + peer, me.h),
                device_id_type=MESH,
            ).start()

        return carry

    lax.fori_loop(0, 16, one, 0)


def await_sends(me, src, dst, send_sem, recv_sem):
    def over(rows):
        pltpu.make_async_remote_copy(
            src_ref=src.at[pl.ds(0, rows)],
            dst_ref=dst.at[pl.ds(0, rows)],
            send_sem=send_sem,
            recv_sem=recv_sem.at[0],
            device_id=me.partner,
            device_id_type=MESH,
        ).wait_send()

    @pl.when(me.has_self)
    def _():
        over(HALF - CELL)

    @pl.when(jnp.logical_not(me.has_self))
    def _():
        over(HALF)


def relay(me, buf, start, rows, send_sem, recv_sem):
    part = buf.at[pl.ds(start, rows)]
    return pltpu.make_async_remote_copy(
        src_ref=part,
        dst_ref=part,
        send_sem=send_sem,
        recv_sem=recv_sem,
        device_id=me.partner,
        device_id_type=MESH,
    )


def local_slots(rank, s):
    return (rank // LENGTH) * CELL + (rank % LENGTH) - s * CELL


def gather_kernel(
    points, rank, gain, w_qkv, w_out, w_fc1, w_fc2,
    q_ref, k_ref, v_ref, raw_ref, w_out_p, w_fc1_p, w_fc2_p,
    acc, send, arrived, send_sem, recv_sem, rsend_sem, rrecv_sem, wsend_sem, wrecv_sem,
):
    me = Place()
    barrier = greet(me)
    slots = local_slots(rank[...], me.s)

    def permute(group):
        first = me.c * HALF + group * GROUP
        total = jnp.zeros((GROUP, FEAT), F32)
        for part in range(4):
            cols = pl.ds(part * 512, 512)
            wanted = first + lax.broadcasted_iota(jnp.int32, (GROUP, 512), 0)
            hit = wanted == slots[:, part * 512 : (part + 1) * 512]
            pick = jnp.where(hit, 1.0, 0.0).astype(BF16)
            total = total + dot(pick, points[cols, :])
        send[pl.ds(pl.multiple_of(group * GROUP, GROUP), GROUP), :] = total.astype(BF16)

    weights = []
    for i, (src, dst) in enumerate(((w_out, w_out_p), (w_fc1, w_fc1_p), (w_fc2, w_fc2_p))):
        weights.append(
            pltpu.make_async_remote_copy(
                src_ref=src,
                dst_ref=dst,
                send_sem=wsend_sem.at[i],
                recv_sem=wrecv_sem.at[i],
                device_id=me.partner,
                device_id_type=MESH,
            )
        )

    for j in range(GROUPS):
        group = me.group(j)
        permute(group)
        if j == 0:
            await_greetings(me, barrier)
        send_group(me, group, send, arrived, send_sem, recv_sem)
    for copy in weights:
        copy.start()

    def project(start):
        rows = pl.ds(start, GROUP)
        normed = norm_rows(arrived[rows, :].astype(F32), gain[...])
        q_ref[rows, :] = (dot(normed, w_qkv[0]) * QSCALE).astype(BF16)
        k_ref[rows, :] = dot(normed, w_qkv[1]).astype(BF16)
        v_ref[rows, :] = dot(normed, w_qkv[2]).astype(BF16)

    def start_of(half, group):
        return pl.multiple_of(half * HALF + group * GROUP, GROUP)

    for j in range(GROUPS):
        group = me.group(j)
        start = start_of(me.c, group)
        copy = relay(me, arrived, start, GROUP, rsend_sem.at[group], recv_sem.at[group])
        copy.wait_recv()
        relay(me, arrived, start, GROUP, rsend_sem.at[group], rrecv_sem.at[group]).start()
        project(start)
    for j in range(GROUPS):
        group = me.group(j)
        start = start_of(1 - me.c, group)
        relay(me, arrived, start, GROUP, rsend_sem.at[group], rrecv_sem.at[group]).wait_recv()
        project(start)
    raw_ref[...] = arrived[pl.ds(pl.multiple_of(me.c * HALF, HALF), HALF), :]
    for j in range(GROUPS):
        group = me.group(j)
        start = start_of(me.c, group)
        relay(me, arrived, start, GROUP, rsend_sem.at[group], rrecv_sem.at[group]).wait_send()
    await_sends(me, send, arrived, send_sem, recv_sem)
    for copy in weights:
        copy.wait()


def attend_kernel(counts, q, k, v, out, qh, kh, vh, scores, highest, total):
    s1 = counts[0, 0]
    s2 = s1 + counts[0, 1]
    s3 = s2 + counts[0, 2]

    def prepare(i, carry):
        rows = pl.ds(pl.multiple_of(i * 256, 256), 256)
        position = i * 256 + lax.broadcasted_iota(jnp.int32, (256, 128), 0)
        lane = lax.broadcasted_iota(jnp.int32, (256, 128), 1)
        patch = (
            (position >= s1).astype(jnp.int32)
            + (position >= s2).astype(jnp.int32)
            + (position >= s3).astype(jnp.int32)
        )
        mark = lane & (HDIM - 1)
        q_mark = jnp.where(mark == patch, 1.0, 0.0).astype(BF16)
        k_mark = jnp.where((mark < 4) & (mark != patch), FAR, 0.0).astype(BF16)
        ones = jnp.ones((256, 128), BF16)
        for head in range(4):
            pair = slice((head // 2) * 128, (head // 2 + 1) * 128)
            own = (lane // HDIM) == (head % 2)
            qh[head, rows, :] = jnp.where(own, q[rows, pair], q_mark)
            kh[head, rows, :] = jnp.where(own, k[rows, pair], k_mark)
            vh[head, rows, :] = jnp.where(own, v[rows, pair], ones)
        return carry

    lax.fori_loop(0, LENGTH // 256, prepare, 0)

    def block(i, carry):
        q0 = i * 256
        last = q0 + 255
        low = jnp.where(q0 >= s3, s3, jnp.where(q0 >= s2, s2, jnp.where(q0 >= s1, s1, 0)))
        high = jnp.where(
            last < s1, s1, jnp.where(last < s2, s2, jnp.where(last < s3, s3, LENGTH))
        )
        first, end = low // 256, (high + 255) // 256
        rows = pl.ds(pl.multiple_of(q0, 256), 256)
        for head in range(4):
            highest[head] = jnp.full((256, 128), -3e38, F32)
            total[head] = jnp.zeros((256, 128), F32)

        def score(j, carry):
            keys = pl.ds(pl.multiple_of(j * 256, 256), 256)
            for head in range(4):
                value = lax.dot_general(
                    qh[head, rows, :],
                    kh[head, keys, :],
                    (((1,), (1,)), ((), ())),
                    preferred_element_type=F32,
                )
                scores[head, j] = value
                highest[head] = jnp.maximum(
                    highest[head], jnp.maximum(value[:, :128], value[:, 128:])
                )
            return carry

        lax.fori_loop(first, end, score, 0)
        for head in range(4):
            highest[head] = jnp.broadcast_to(
                jnp.max(highest[head], axis=-1, keepdims=True), (256, 128)
            )

        def weigh(j, carry):
            keys = pl.ds(pl.multiple_of(j * 256, 256), 256)
            for head in range(4):
                top = highest[head]
                value = scores[head, j]
                raised = jnp.concatenate(
                    [jnp.exp2(value[:, :128] - top), jnp.exp2(value[:, 128:] - top)], axis=1
                ).astype(BF16)
                total[head] += dot(raised, vh[head, keys, :])
            return carry

        lax.fori_loop(first, end, weigh, 0)
        lane = lax.broadcasted_iota(jnp.int32, (256, 128), 1)
        for pair in range(2):
            done = []
            for head in (2 * pair, 2 * pair + 1):
                value = total[head]
                done.append(value / pltpu.roll(value, HDIM, 1))
            out[rows, pair * 128 : (pair + 1) * 128] = jnp.where(
                lane < HDIM, done[0], done[1]
            ).astype(BF16)
        return carry

    lax.fori_loop(0, LENGTH // 256, block, 0)


def return_kernel(
    ctx, raw, gain, w_out, w_fc1, w_fc2, w_out_p, w_fc1_p, w_fc2_p,
    back_ref, ctx_p, send, send_sem, recv_sem, rsend_sem, rrecv_sem, csend_sem, crecv_sem,
):
    me = Place()
    barrier = greet(me)
    await_greetings(me, barrier)
    own_half = pl.multiple_of(me.c * HALF, HALF)
    other_half = pl.multiple_of((1 - me.c) * HALF, HALF)
    swap = pltpu.make_async_remote_copy(
        src_ref=ctx.at[pl.ds(other_half, HALF)],
        dst_ref=ctx_p,
        send_sem=csend_sem,
        recv_sem=crecv_sem,
        device_id=me.partner,
        device_id_type=MESH,
    )
    swap.start()
    swap.wait_recv()

    def finish(group):
        start = pl.multiple_of(group * GROUP, GROUP)
        rows = pl.ds(start, GROUP)
        own_rows = pl.ds(pl.multiple_of(own_half + start, GROUP), GROUP)
        attn = dot(ctx[own_rows, :], w_out[...]) + dot(ctx_p[rows, :], w_out_p[...])
        middle = (raw[rows, :].astype(F32) + attn.astype(BF16).astype(F32)).astype(BF16).astype(F32)
        normed = norm_rows(middle, gain[...])
        result = middle
        for fc1, fc2 in ((w_fc1, w_fc2), (w_fc1_p, w_fc2_p)):
            hidden = jax.nn.gelu(dot(normed, fc1[...]), approximate=True).astype(BF16)
            result = result + dot(hidden, fc2[...])
        send[rows, :] = result.astype(BF16)

    for j in range(GROUPS):
        group = me.group(j)
        finish(group)
        send_group(me, group, send, back_ref, send_sem, recv_sem)

    def start_of(half, group):
        return pl.multiple_of(half * HALF + group * GROUP, GROUP)

    for j in range(GROUPS):
        group = me.group(j)
        start = start_of(me.c, group)
        relay(me, back_ref, start, GROUP, rsend_sem.at[group], recv_sem.at[group]).wait_recv()
        relay(me, back_ref, start, GROUP, rsend_sem.at[group], rrecv_sem.at[group]).start()
    for j in range(GROUPS):
        group = me.group(j)
        start = start_of(1 - me.c, group)
        relay(me, back_ref, start, GROUP, rsend_sem.at[group], rrecv_sem.at[group]).wait_recv()
    for j in range(GROUPS):
        group = me.group(j)
        start = start_of(me.c, group)
        relay(me, back_ref, start, GROUP, rsend_sem.at[group], rrecv_sem.at[group]).wait_send()
    swap.wait_send()
    await_sends(me, send, back_ref, send_sem, recv_sem)


def place_kernel(rank, back, out):
    s = lax.axis_index("space")
    i = pl.program_id(0)
    slots = local_slots(rank[...], s)
    total = jnp.zeros((256, FEAT), F32)
    columns = [
        jnp.broadcast_to(slots[:, p * 128 : (p + 1) * 128], (128, 128)).T for p in range(2)
    ]
    column = jnp.concatenate(columns, axis=0)
    lane = lax.broadcasted_iota(jnp.int32, (256, 128), 1)
    for part in range(4):
        picks = [
            jnp.where(column == lane + (part * 512 + t * 128), 1.0, 0.0).astype(BF16)
            for t in range(4)
        ]
        total = total + dot(jnp.concatenate(picks, axis=1), back[pl.ds(part * 512, 512), :])
    out[...] = total.astype(BF16)


def body(
    points, curve_rank, patch_counts, norm_gain_attn, w_qkv, w_out, norm_gain_mlp, w_fc1, w_fc2
):
    rank = curve_rank.reshape(1, LENGTH)
    shape = jax.ShapeDtypeStruct
    vm = pl.BlockSpec(memory_space=pltpu.VMEM)
    anywhere = pl.BlockSpec(memory_space=pl.ANY)
    dma = pltpu.SemaphoreType.DMA
    cols = w_qkv.shape[2]
    q, k, v, raw, w_out_p, w_fc1_p, w_fc2_p = pl.pallas_call(
        gather_kernel,
        name="gather_rows",
        out_shape=(
            shape((LENGTH, cols), BF16),
            shape((LENGTH, cols), BF16),
            shape((LENGTH, cols), BF16),
            shape((HALF, FEAT), BF16),
            shape(w_out.shape, BF16),
            shape(w_fc1.shape, BF16),
            shape(w_fc2.shape, BF16),
        ),
        in_specs=[vm] * 4 + [anywhere] * 3,
        out_specs=[vm] * 4 + [anywhere] * 3,
        scratch_shapes=[
            VMEM((GROUP, FEAT), F32),
            VMEM((HALF, FEAT), BF16),
            VMEM((LENGTH, FEAT), BF16),
            dma, dma((4,)), dma((4,)), dma((4,)), dma((3,)), dma((3,)),
        ],
        compiler_params=pltpu.CompilerParams(collective_id=0, has_side_effects=True),
    )(points, rank, norm_gain_attn.reshape(1, FEAT), w_qkv, w_out, w_fc1, w_fc2)

    context = pl.pallas_call(
        attend_kernel,
        name="attend",
        out_shape=shape((LENGTH, cols), BF16),
        in_specs=[pl.BlockSpec(memory_space=pltpu.SMEM)] + [vm] * 3,
        out_specs=vm,
        scratch_shapes=[
            VMEM((4, LENGTH, 128), BF16),
            VMEM((4, LENGTH, 128), BF16),
            VMEM((4, LENGTH, 128), BF16),
            VMEM((4, 8, 256, 256), F32),
            VMEM((4, 256, 128), F32),
            VMEM((4, 256, 128), F32),
        ],
    )(patch_counts, q, k, v)

    back = pl.pallas_call(
        return_kernel,
        name="return_rows",
        out_shape=shape((LENGTH, FEAT), BF16),
        in_specs=[vm] * 9,
        out_specs=vm,
        scratch_shapes=[
            VMEM((HALF, cols), BF16),
            VMEM((HALF, FEAT), BF16),
            dma, dma((4,)), dma((4,)), dma((4,)), dma, dma,
        ],
        compiler_params=pltpu.CompilerParams(collective_id=1, has_side_effects=True),
    )(context, raw, norm_gain_mlp.reshape(1, FEAT), w_out, w_fc1, w_fc2, w_out_p, w_fc1_p, w_fc2_p)

    return pl.pallas_call(
        place_kernel,
        name="place_rows",
        grid=(LENGTH // 256,),
        out_shape=shape((LENGTH, FEAT), BF16),
        in_specs=[
            pl.BlockSpec((1, 256), lambda i: (0, i)),
            pl.BlockSpec((LENGTH, FEAT), lambda i: (0, 0)),
        ],
        out_specs=pl.BlockSpec((256, FEAT), lambda i: (i, 0)),
    )(rank, back)


def solution(mesh):
    placed = (
        P("space", None),
        P("space"),
        P("space", None),
        P(),
        P(None, None, "mp"),
        P("mp", None),
        P(),
        P(None, "mp"),
        P("mp", None),
    )
    return jax.shard_map(
        body, mesh=mesh, in_specs=placed, out_specs=P("space", None), check_vma=False
    )
```

```python
import functools
import math

import jax
import jax.numpy as jnp
from jax import lax
from jax.experimental import pallas as pl
from jax.experimental.pallas import tpu as pltpu
from jax.sharding import PartitionSpec as P

HDIM = 64
EPS = 1e-06
FAR = -1e30
QSCALE = math.log2(math.e) / math.sqrt(HDIM)

LENGTH = 2048
FEAT = 512
HALF = 1024
SHARDS = 128
PEERS = 64
CELL = 16
GROUP = 256
GROUPS = 4
NX, NZ = 4, 8

MESH = pl.DeviceIdType.MESH
VMEM = pltpu.VMEM
F32 = jnp.float32
BF16 = jnp.bfloat16


def dot(a, b):
    return jnp.dot(a, b, preferred_element_type=F32)


def norm_rows(values, gain):
    average = jnp.mean(values, axis=-1, keepdims=True)
    centred = values - average
    second = jnp.mean(centred * centred, axis=-1, keepdims=True)
    return (centred * lax.rsqrt(second + EPS) * gain).astype(BF16)


class Place:
    def __init__(self):
        self.s = lax.axis_index("space")
        self.c = lax.axis_index("mp")
        self.x = lax.rem(self.s, NX)
        self.z = lax.rem(self.s // NX, NZ)
        self.h = self.s // PEERS
        self.own = self.s - self.h * PEERS
        self.partner = (self.s, 1 - self.c)
        self.has_self = self.h == self.c

    def group(self, j):
        near = self.z // (NZ // 2)
        zh = (1 - near) if j < 2 else near
        return (j % 2) * 2 + zh

    def peer(self, group, q):
        zz = lax.rem(q // NX + self.z, NZ // 2)
        xx = lax.rem(q + self.x, NX)
        return group * 16 + zz * NX + xx


def greet(me):
    barrier = pltpu.get_barrier_semaphore()

    def one(i, carry):
        peer = lax.rem(me.own + i, PEERS)

        @pl.when(jnp.logical_not(me.has_self & (i == 0)))
        def _():
            pl.semaphore_signal(
                barrier, inc=1, device_id=(me.c * PEERS + peer, me.h), device_id_type=MESH
            )

        return carry

    lax.fori_loop(0, PEERS, one, 0)
    pl.semaphore_signal(barrier, inc=1, device_id=me.partner, device_id_type=MESH)
    return barrier


def await_greetings(me, barrier):
    pl.semaphore_wait(barrier, jnp.where(me.has_self, PEERS, PEERS + 1))


def send_group(me, group, src, dst, at, send_sem, recv_sem):
    landing = pl.multiple_of(at * CELL, CELL)
    mine = me.own // 16

    def one(q, carry):
        peer = me.peer(group, q)
        rows = pl.ds(pl.multiple_of(peer * CELL, CELL), CELL)
        itself = me.has_self & (peer == me.own)

        @pl.when(itself)
        def _():
            pltpu.make_async_copy(
                src.at[rows], dst.at[pl.ds(landing, CELL)], recv_sem.at[mine]
            ).start()

        @pl.when(jnp.logical_not(itself))
        def _():
            pltpu.make_async_remote_copy(
                src_ref=src.at[rows],
                dst_ref=dst.at[pl.ds(landing, CELL)],
                send_sem=send_sem,
                recv_sem=recv_sem.at[mine],
                device_id=(me.c * PEERS + peer, me.h),
                device_id_type=MESH,
            ).start()

        return carry

    lax.fori_loop(0, 16, one, 0)


def await_sends(me, src, dst, send_sem, recv_sem):
    def over(rows):
        pltpu.make_async_remote_copy(
            src_ref=src.at[pl.ds(0, rows)],
            dst_ref=dst.at[pl.ds(0, rows)],
            send_sem=send_sem,
            recv_sem=recv_sem.at[0],
            device_id=me.partner,
            device_id_type=MESH,
        ).wait_send()

    @pl.when(me.has_self)
    def _():
        over(HALF - CELL)

    @pl.when(jnp.logical_not(me.has_self))
    def _():
        over(HALF)


def relay(me, buf, start, rows, send_sem, recv_sem):
    part = buf.at[pl.ds(start, rows)]
    return pltpu.make_async_remote_copy(
        src_ref=part,
        dst_ref=part,
        send_sem=send_sem,
        recv_sem=recv_sem,
        device_id=me.partner,
        device_id_type=MESH,
    )


def local_slots(rank, s):
    return (rank // LENGTH) * CELL + (rank % LENGTH) - s * CELL


WIN = 1152
KEYS = 384
ITEMS = 11


def layer_kernel(
    points, rank, counts, gain_attn, w_qkv, w_out, gain_mlp, w_fc1, w_fc2,
    back,
    send, arrived, wq, wo, f1, f2, kk, marks, vt, qt, ctxv, s0, s1, p0, p1, m0, m1, table,
    send_sem, recv_sem, wloc_sem, wsend_sem, wrecv_sem, ksend_sem, krecv_sem,
    vsend_sem, vrecv_sem, bsend_sem, brecv_sem, rsend_sem, rrecv_sem,
):
    me = Place()
    barrier = greet(me)
    slots = local_slots(rank[...], me.s)
    s_refs, p_refs, m_refs = (s0, s1), (p0, p1), (m0, m1)

    def permute(group):
        first = me.c * HALF + group * GROUP
        total = jnp.zeros((GROUP, FEAT), F32)
        for part in range(4):
            wanted = first + lax.broadcasted_iota(jnp.int32, (GROUP, 512), 0)
            hit = wanted == slots[:, part * 512 : (part + 1) * 512]
            pick = jnp.where(hit, 1.0, 0.0).astype(BF16)
            total = total + dot(pick, points[pl.ds(part * 512, 512), :])
        send[pl.ds(pl.multiple_of(group * GROUP, GROUP), GROUP), :] = total.astype(BF16)

    local, remote = [], []
    for i, (src, dst) in enumerate(((w_qkv, wq), (w_out, wo), (w_fc1, f1), (w_fc2, f2))):
        copy = pltpu.make_async_copy(src, dst.at[me.c], wloc_sem.at[i])
        copy.start()
        local.append(copy)
        remote.append(
            pltpu.make_async_remote_copy(
                src_ref=src,
                dst_ref=dst.at[me.c],
                send_sem=wsend_sem.at[i],
                recv_sem=wrecv_sem.at[i],
                device_id=me.partner,
                device_id_type=MESH,
            )
        )

    for j in range(GROUPS):
        group = me.group(j)
        permute(group)
        if j == 0:
            await_greetings(me, barrier)
            remote[0].start()
        send_group(me, group, send, arrived, me.own, send_sem, recv_sem)
    for copy in remote[1:]:
        copy.start()

    c1 = counts[0, 0]
    c2 = c1 + counts[0, 1]
    c3 = c2 + counts[0, 2]

    def patch_of(position):
        return (
            (position >= c1).astype(jnp.int32)
            + (position >= c2).astype(jnp.int32)
            + (position >= c3).astype(jnp.int32)
        )

    def mark_keys(i, carry):
        patch = patch_of(i * 128 + lax.broadcasted_iota(jnp.int32, (128, 128), 0))
        lane = lax.broadcasted_iota(jnp.int32, (128, 128), 1)
        marks[i] = jnp.where((lane < 4) & (lane != patch), FAR, 0.0).astype(BF16)
        for pair in range(4):
            vt[pair, i, 128:144, :] = jnp.ones((16, 128), BF16)
        return carry

    lax.fori_loop(0, LENGTH // 128, mark_keys, 0)

    def mark_queries(i, carry):
        first = me.c * HALF + i * 128
        patch = patch_of(first + lax.broadcasted_iota(jnp.int32, (128, 256), 1) % 128)
        row = lax.broadcasted_iota(jnp.int32, (128, 256), 0)
        mark = jnp.where(row == patch, 1.0, 0.0).astype(BF16)
        for pair in range(4):
            qt[i, pair, 128:256, :] = mark
        return carry

    lax.fori_loop(0, 8, mark_queries, 0)

    upward = me.z // (NZ // 2)

    def in_stream(n, count):
        return upward * n + (1 - upward) * (count - 1 - n)

    zero = c1 * 0
    firsts, lasts, begins, index = [], [], [], zero
    for n in range(8):
        row = me.c * HALF + in_stream(n, 8) * 128
        firsts.append(patch_of(row))
        lasts.append(patch_of(row + 127))
        begins.append(index)
        index = index + lasts[n] - firsts[n] + 1
        table[2, n] = begins[n]
        table[3, n] = firsts[n]
    for i in range(ITEMS + 1):
        block, patch = in_stream(0, 8), jnp.minimum(firsts[0] + i, lasts[0])
        for n in range(1, 8):
            reached = begins[n] <= i
            block = jnp.where(reached, in_stream(n, 8), block)
            patch = jnp.where(
                reached, jnp.minimum(firsts[n] + i - begins[n], lasts[n]), patch
            )
        start = jnp.where(
            patch >= 3, c3, jnp.where(patch >= 2, c2, jnp.where(patch >= 1, c1, zero))
        )
        table[0, i + 1] = block
        table[1, i + 1] = jnp.minimum(start // 128, (LENGTH - WIN) // 128)

    local[0].wait()
    remote[0].wait_recv()

    def project(group):
        rows = pl.ds(pl.multiple_of(group * GROUP, GROUP), GROUP)
        place = me.c * 8 + group * 2
        normed = norm_rows(arrived[rows, :].astype(F32), gain_attn[...])
        row = lax.broadcasted_iota(jnp.int32, (128, 128), 0)
        for half in range(2):
            keys = dot(normed, wq[half, 1]).astype(BF16)
            values = dot(normed, wq[half, 2])
            for p in range(2):
                pair, cols = 2 * half + p, slice(p * 128, (p + 1) * 128)
                for b in range(2):
                    kk[pair, place + b] = keys[b * 128 : (b + 1) * 128, cols]
                    vt[pair, place + b, 0:128, :] = values[b * 128 : (b + 1) * 128, cols].T.astype(
                        BF16
                    )
        for half in range(2):
            queries = dot(normed, wq[half, 0]) * QSCALE
            for p in range(2):
                pair, cols = 2 * half + p, slice(p * 128, (p + 1) * 128)
                for b in range(2):
                    turned = queries[b * 128 : (b + 1) * 128, cols].T
                    block = group * 2 + b
                    qt[block, pair, 0:128, 0:128] = jnp.where(row < HDIM, turned, 0.0).astype(BF16)
                    qt[block, pair, 0:128, 128:256] = jnp.where(row >= HDIM, turned, 0.0).astype(
                        BF16
                    )

    def exchange(half, group):
        place = half * 8 + group * 2
        k_part = kk.at[:, pl.ds(place, 2)]
        v_part = vt.at[:, pl.ds(place, 2), pl.ds(0, 128)]
        return [
            pltpu.make_async_remote_copy(
                src_ref=part,
                dst_ref=part,
                send_sem=ss.at[group],
                recv_sem=rs.at[group],
                device_id=me.partner,
                device_id_type=MESH,
            )
            for part, ss, rs in (
                (k_part, ksend_sem, krecv_sem),
                (v_part, vsend_sem, vrecv_sem),
            )
        ]

    for j in range(GROUPS):
        group = me.group(j)
        relay(
            me, arrived, pl.multiple_of(group * GROUP, GROUP), GROUP,
            rsend_sem.at[group], recv_sem.at[group],
        ).wait_recv()
        project(group)
        for copy in exchange(me.c, group):
            copy.start()
    await_sends(me, send, arrived, send_sem, recv_sem)
    for i in range(1, 4):
        local[i].wait()
        remote[i].wait_recv()
    for j in range(GROUPS):
        for copy in exchange(1 - me.c, me.group(j)):
            copy.wait_recv()

    def score(pair, item, part, dst, top):
        keys = pl.ds(table[1, item] + part * (KEYS // 128), KEYS // 128)
        lhs = jnp.concatenate([kk[pair, keys], marks[keys]], axis=2).reshape(KEYS, 256)
        value = dot(lhs, qt[table[0, item], pair])
        s_refs[dst][part * KEYS : (part + 1) * KEYS, :] = value
        high = jnp.max(value.reshape(KEYS // 8, 8, 256), axis=0)
        return high if top is None else jnp.maximum(top, high)

    def settle(dst, top):
        m_refs[dst][...] = jnp.broadcast_to(jnp.max(top, axis=0, keepdims=True), (8, 256))

    def raise_part(src, part, top):
        rows = slice(part * 128, (part + 1) * 128)
        p_refs[src][rows, :] = jnp.exp2(s_refs[src][rows, :] - top).astype(BF16)

    def weigh(pair, item, src, low, count, total):
        start = table[1, item] + low // 128
        lhs = [vt[pair, start + b] for b in range(count // 128)]
        lhs = jnp.concatenate(lhs, axis=1) if count > 128 else lhs[0]
        value = dot(lhs, p_refs[src][low : low + count, :])
        return value if total is None else total + value

    def conclude(pair, item, total):
        inverse = 1.0 / total[128:129, :]
        result = jnp.concatenate(
            [
                total[0:64, 0:128] * inverse[:, 0:128],
                total[64:128, 128:256] * inverse[:, 128:256],
            ],
            axis=0,
        )
        ctxv[item, :, pair * 128 : (pair + 1) * 128] = result.T.astype(BF16)

    def step(item, pair):
        now, other = pair % 2, 1 - pair % 2
        after, after_pair = (item, pair + 1) if pair < 3 else (item + 1, 0)
        before, before_pair = (item, pair - 1) if pair > 0 else (item - 1, 3)
        top = m_refs[now][0:1, :]
        high = total = None
        for part in range(9):
            if part % 3 == 0:
                high = score(after_pair, after, part // 3, other, high)
            raise_part(now, part, top)
            if part % 2 == 1:
                total = weigh(before_pair, before, other, (part - 1) * 128, 256, total)
        total = weigh(before_pair, before, other, 1024, 128, total)
        conclude(before_pair, before, total)
        settle(other, high)

    def one_item(item, carry):
        for pair in range(4):
            step(item, pair)
        return carry

    table[0, 0] = table[0, 1]
    table[1, 0] = table[1, 1]
    p1[...] = jnp.zeros_like(p1)
    high = None
    for part in range(3):
        high = score(0, 1, part, 0, high)
    settle(0, high)

    def block_context(n):
        begin, first = table[2, n] + 1, table[3, n]
        row = me.c * HALF + in_stream(n, 8) * 128
        nth = patch_of(row + lax.broadcasted_iota(jnp.int32, (128, FEAT), 0)) - first
        value = ctxv[begin]
        for e in range(1, 4):
            value = jnp.where(nth >= e, ctxv[jnp.minimum(begin + e, ITEMS)], value)
        return value

    def finish(j):
        group = in_stream(j, GROUPS)
        low, high = 2 * j + 1 - upward, 2 * j + upward
        ctx = jnp.concatenate([block_context(low), block_context(high)], axis=0)
        rows = pl.ds(pl.multiple_of(group * GROUP, GROUP), GROUP)
        attn = dot(ctx[:, :256], wo[0]) + dot(ctx[:, 256:], wo[1])
        middle = (arrived[rows, :].astype(F32) + attn.astype(BF16).astype(F32)).astype(BF16)
        middle = middle.astype(F32)
        normed = norm_rows(middle, gain_mlp[...])
        result = middle
        for half in range(2):
            hidden = jax.nn.gelu(dot(normed, f1[half]), approximate=True).astype(BF16)
            result = result + dot(hidden, f2[half])
        send[rows, :] = result.astype(BF16)
        send_group(me, group, send, back, me.s, bsend_sem, brecv_sem)

    def stretch(j, carry):
        low = jnp.where(j == 0, 1, 2 * j + 4)
        high = 2 * j + 6
        lax.fori_loop(low, high, one_item, 0)
        total = None
        for part in range(4):
            total = weigh(3, high - 1, 1, part * 256, 256, total)
        conclude(3, high - 1, weigh(3, high - 1, 1, 1024, 128, total))
        finish(j)
        return carry

    lax.fori_loop(0, GROUPS, stretch, 0)

    early = jnp.where(me.own // 16 < 2, 1, 0)
    order = [early, early + 2, 1 - early, 3 - early]

    def passing(half, group, recv):
        start = pl.multiple_of(half * HALF + group * GROUP, GROUP)
        return relay(me, back, start, GROUP, rsend_sem.at[group], recv.at[group])

    for group in order:
        passing(me.c, group, brecv_sem).wait_recv()
        passing(me.c, group, rrecv_sem).start()
    for group in order:
        passing(1 - me.c, group, rrecv_sem).wait_recv()
    for group in order:
        passing(me.c, group, rrecv_sem).wait_send()
    await_sends(me, send, back, bsend_sem, brecv_sem)
    for j in range(GROUPS):
        for copy in exchange(me.c, me.group(j)):
            copy.wait_send()
    for copy in remote:
        copy.wait_send()


def place_kernel(rank, back, out):
    s = lax.axis_index("space")
    i = pl.program_id(0)
    slots = local_slots(rank[...], s)
    total = jnp.zeros((256, FEAT), F32)
    columns = [
        jnp.broadcast_to(slots[:, p * 128 : (p + 1) * 128], (128, 128)).T for p in range(2)
    ]
    column = jnp.concatenate(columns, axis=0)
    lane = lax.broadcasted_iota(jnp.int32, (256, 128), 1)
    for part in range(4):
        picks = [
            jnp.where(column == lane + (part * 512 + t * 128), 1.0, 0.0).astype(BF16)
            for t in range(4)
        ]
        total = total + dot(jnp.concatenate(picks, axis=1), back[pl.ds(part * 512, 512), :])
    out[...] = total.astype(BF16)


def body(
    points, curve_rank, patch_counts, norm_gain_attn, w_qkv, w_out, norm_gain_mlp, w_fc1, w_fc2
):
    rank = curve_rank.reshape(1, LENGTH)
    shape = jax.ShapeDtypeStruct
    vm = pl.BlockSpec(memory_space=pltpu.VMEM)
    anywhere = pl.BlockSpec(memory_space=pl.ANY)
    dma = pltpu.SemaphoreType.DMA
    back = pl.pallas_call(
        layer_kernel,
        name="layer",
        out_shape=shape((LENGTH, FEAT), BF16),
        in_specs=[vm, vm, pl.BlockSpec(memory_space=pltpu.SMEM), vm, anywhere, anywhere, vm]
        + [anywhere] * 2,
        out_specs=vm,
        scratch_shapes=[
            VMEM((HALF, FEAT), BF16),
            VMEM((HALF, FEAT), BF16),
            VMEM((2,) + w_qkv.shape, BF16),
            VMEM((2,) + w_out.shape, BF16),
            VMEM((2,) + w_fc1.shape, BF16),
            VMEM((2,) + w_fc2.shape, BF16),
            VMEM((4, 16, 128, 128), BF16),
            VMEM((16, 128, 128), BF16),
            VMEM((4, 16, 144, 128), BF16),
            VMEM((8, 4, 256, 256), BF16),
            VMEM((ITEMS + 1, 128, FEAT), BF16),
            VMEM((WIN, 256), F32),
            VMEM((WIN, 256), F32),
            VMEM((WIN, 256), BF16),
            VMEM((WIN, 256), BF16),
            VMEM((8, 256), F32),
            VMEM((8, 256), F32),
            pltpu.SMEM((4, 16), jnp.int32),
            dma, dma((4,)), dma((4,)), dma((4,)), dma((4,)), dma((4,)), dma((4,)),
            dma((4,)), dma((4,)), dma, dma((4,)), dma((4,)), dma((4,)),
        ],
        compiler_params=pltpu.CompilerParams(collective_id=0, has_side_effects=True),
    )(
        points, rank, patch_counts, norm_gain_attn.reshape(1, FEAT), w_qkv, w_out,
        norm_gain_mlp.reshape(1, FEAT), w_fc1, w_fc2,
    )

    return pl.pallas_call(
        place_kernel,
        name="place_rows",
        grid=(LENGTH // 256,),
        out_shape=shape((LENGTH, FEAT), BF16),
        in_specs=[
            pl.BlockSpec((1, 256), lambda i: (0, i)),
            pl.BlockSpec((LENGTH, FEAT), lambda i: (0, 0)),
        ],
        out_specs=pl.BlockSpec((256, FEAT), lambda i: (i, 0)),
    )(rank, back)


def solution(mesh):
    placed = (
        P("space", None),
        P("space"),
        P("space", None),
        P(),
        P(None, None, "mp"),
        P("mp", None),
        P(),
        P(None, "mp"),
        P("mp", None),
    )
    return jax.shard_map(
        body, mesh=mesh, in_specs=placed, out_specs=P("space", None), check_vma=False
    )
```

```python
import functools
import math

import jax
import jax.numpy as jnp
from jax import lax
from jax.experimental import pallas as pl
from jax.experimental.pallas import tpu as pltpu
from jax.sharding import PartitionSpec as P

HDIM = 64
EPS = 1e-06
FAR = -1e30
QSCALE = math.log2(math.e) / math.sqrt(HDIM)

LENGTH = 2048
FEAT = 512
HALF = 1024
SHARDS = 128
PEERS = 64
CELL = 16
GROUP = 256
GROUPS = 4
NX, NZ = 4, 8

MESH = pl.DeviceIdType.MESH
VMEM = pltpu.VMEM
F32 = jnp.float32
BF16 = jnp.bfloat16


def dot(a, b):
    return jnp.dot(a, b, preferred_element_type=F32)


def norm_rows(values, gain):
    average = jnp.mean(values, axis=-1, keepdims=True)
    centred = values - average
    second = jnp.mean(centred * centred, axis=-1, keepdims=True)
    return (centred * lax.rsqrt(second + EPS) * gain).astype(BF16)


class Place:
    def __init__(self):
        self.s = lax.axis_index("space")
        self.c = lax.axis_index("mp")
        self.x = lax.rem(self.s, NX)
        self.z = lax.rem(self.s // NX, NZ)
        self.h = self.s // PEERS
        self.own = self.s - self.h * PEERS
        self.partner = (self.s, 1 - self.c)
        self.has_self = self.h == self.c

    def group(self, j):
        near = self.z // (NZ // 2)
        zh = (1 - near) if j < 2 else near
        return (j % 2) * 2 + zh

    def peer(self, group, q):
        zz = lax.rem(q // NX + self.z, NZ // 2)
        xx = lax.rem(q + self.x, NX)
        return group * 16 + zz * NX + xx


def greet(me):
    barrier = pltpu.get_barrier_semaphore()

    def one(i, carry):
        peer = lax.rem(me.own + i, PEERS)

        @pl.when(jnp.logical_not(me.has_self & (i == 0)))
        def _():
            pl.semaphore_signal(
                barrier, inc=1, device_id=(me.c * PEERS + peer, me.h), device_id_type=MESH
            )

        return carry

    lax.fori_loop(0, PEERS, one, 0)
    pl.semaphore_signal(barrier, inc=1, device_id=me.partner, device_id_type=MESH)
    return barrier


def await_greetings(me, barrier):
    pl.semaphore_wait(barrier, jnp.where(me.has_self, PEERS, PEERS + 1))


def send_group(me, group, src, dst, at, send_sem, recv_sem):
    landing = pl.multiple_of(at * CELL, CELL)
    mine = me.own // 16

    def one(q, carry):
        peer = me.peer(group, q)
        rows = pl.ds(pl.multiple_of(peer * CELL, CELL), CELL)
        itself = me.has_self & (peer == me.own)

        @pl.when(itself)
        def _():
            pltpu.make_async_copy(
                src.at[rows], dst.at[pl.ds(landing, CELL)], recv_sem.at[mine]
            ).start()

        @pl.when(jnp.logical_not(itself))
        def _():
            pltpu.make_async_remote_copy(
                src_ref=src.at[rows],
                dst_ref=dst.at[pl.ds(landing, CELL)],
                send_sem=send_sem,
                recv_sem=recv_sem.at[mine],
                device_id=(me.c * PEERS + peer, me.h),
                device_id_type=MESH,
            ).start()

        return carry

    lax.fori_loop(0, 16, one, 0)


def await_sends(me, src, dst, send_sem, recv_sem):
    def over(rows):
        pltpu.make_async_remote_copy(
            src_ref=src.at[pl.ds(0, rows)],
            dst_ref=dst.at[pl.ds(0, rows)],
            send_sem=send_sem,
            recv_sem=recv_sem.at[0],
            device_id=me.partner,
            device_id_type=MESH,
        ).wait_send()

    @pl.when(me.has_self)
    def _():
        over(HALF - CELL)

    @pl.when(jnp.logical_not(me.has_self))
    def _():
        over(HALF)


def relay(me, buf, start, rows, send_sem, recv_sem):
    part = buf.at[pl.ds(start, rows)]
    return pltpu.make_async_remote_copy(
        src_ref=part,
        dst_ref=part,
        send_sem=send_sem,
        recv_sem=recv_sem,
        device_id=me.partner,
        device_id_type=MESH,
    )


def local_slots(rank, s):
    return (rank // LENGTH) * CELL + (rank % LENGTH) - s * CELL


def early_groups(me):
    return jnp.where(me.own // 16 < 2, 1, 0)


def group_bases(parity):
    return [
        pl.multiple_of(half * HALF + (parity + 2 * k) * GROUP, GROUP)
        for half in range(2)
        for k in range(2)
    ]


def slot_column(slots):
    return jnp.concatenate(
        [
            jnp.broadcast_to(slots[:, p * 128 : (p + 1) * 128], (128, 128)).T
            for p in range(slots.shape[1] // 128)
        ],
        axis=0,
    )


def picks(column, base):
    lane = lax.broadcasted_iota(jnp.int32, column.shape, 1)
    return jnp.concatenate(
        [
            jnp.where(column == lane + (base + t * 128), 1.0, 0.0).astype(BF16)
            for t in range(GROUP // 128)
        ],
        axis=1,
    )


WIN = 1152
KEYS = 384
ITEMS = 11


def layer_kernel(
    points, rank, counts, gain_attn, w_qkv, w_out, gain_mlp, w_fc1, w_fc2,
    part_ref, late_ref,
    back, placed, send, arrived, wq, wo, f1, f2, kk, marks, vt, qt, ctxv, s0, s1, p0, p1, m0, m1, table,
    send_sem, recv_sem, wloc_sem, wsend_sem, wrecv_sem, ksend_sem, krecv_sem,
    vsend_sem, vrecv_sem, bsend_sem, brecv_sem, rsend_sem, rrecv_sem,
    out_sem,
):
    me = Place()
    barrier = greet(me)
    slots = local_slots(rank[...], me.s)
    s_refs, p_refs, m_refs = (s0, s1), (p0, p1), (m0, m1)

    def permute(group):
        first = me.c * HALF + group * GROUP
        total = jnp.zeros((GROUP, FEAT), F32)
        for part in range(4):
            wanted = first + lax.broadcasted_iota(jnp.int32, (GROUP, 512), 0)
            hit = wanted == slots[:, part * 512 : (part + 1) * 512]
            pick = jnp.where(hit, 1.0, 0.0).astype(BF16)
            total = total + dot(pick, points[pl.ds(part * 512, 512), :])
        send[pl.ds(pl.multiple_of(group * GROUP, GROUP), GROUP), :] = total.astype(BF16)

    local, remote = [], []
    for i, (src, dst) in enumerate(((w_qkv, wq), (w_out, wo), (w_fc1, f1), (w_fc2, f2))):
        copy = pltpu.make_async_copy(src, dst.at[me.c], wloc_sem.at[i])
        copy.start()
        local.append(copy)
        remote.append(
            pltpu.make_async_remote_copy(
                src_ref=src,
                dst_ref=dst.at[me.c],
                send_sem=wsend_sem.at[i],
                recv_sem=wrecv_sem.at[i],
                device_id=me.partner,
                device_id_type=MESH,
            )
        )

    for j in range(GROUPS):
        group = me.group(j)
        permute(group)
        if j == 0:
            await_greetings(me, barrier)
            remote[0].start()
        send_group(me, group, send, arrived, me.own, send_sem, recv_sem)
    for copy in remote[1:]:
        copy.start()

    c1 = counts[0, 0]
    c2 = c1 + counts[0, 1]
    c3 = c2 + counts[0, 2]

    def patch_of(position):
        return (
            (position >= c1).astype(jnp.int32)
            + (position >= c2).astype(jnp.int32)
            + (position >= c3).astype(jnp.int32)
        )

    def mark_keys(i, carry):
        patch = patch_of(i * 128 + lax.broadcasted_iota(jnp.int32, (128, 128), 0))
        lane = lax.broadcasted_iota(jnp.int32, (128, 128), 1)
        marks[i] = jnp.where((lane < 4) & (lane != patch), FAR, 0.0).astype(BF16)
        for pair in range(4):
            vt[pair, i, 128:144, :] = jnp.ones((16, 128), BF16)
        return carry

    lax.fori_loop(0, LENGTH // 128, mark_keys, 0)

    def mark_queries(i, carry):
        first = me.c * HALF + i * 128
        patch = patch_of(first + lax.broadcasted_iota(jnp.int32, (128, 256), 1) % 128)
        row = lax.broadcasted_iota(jnp.int32, (128, 256), 0)
        mark = jnp.where(row == patch, 1.0, 0.0).astype(BF16)
        for pair in range(4):
            qt[i, pair, 128:256, :] = mark
        return carry

    lax.fori_loop(0, 8, mark_queries, 0)

    upward = me.z // (NZ // 2)

    def in_stream(n, count):
        return upward * n + (1 - upward) * (count - 1 - n)

    zero = c1 * 0
    firsts, lasts, begins, index = [], [], [], zero
    for n in range(8):
        row = me.c * HALF + in_stream(n, 8) * 128
        firsts.append(patch_of(row))
        lasts.append(patch_of(row + 127))
        begins.append(index)
        index = index + lasts[n] - firsts[n] + 1
        table[2, n] = begins[n]
        table[3, n] = firsts[n]
    for i in range(ITEMS + 1):
        block, patch = in_stream(0, 8), jnp.minimum(firsts[0] + i, lasts[0])
        for n in range(1, 8):
            reached = begins[n] <= i
            block = jnp.where(reached, in_stream(n, 8), block)
            patch = jnp.where(
                reached, jnp.minimum(firsts[n] + i - begins[n], lasts[n]), patch
            )
        start = jnp.where(
            patch >= 3, c3, jnp.where(patch >= 2, c2, jnp.where(patch >= 1, c1, zero))
        )
        table[0, i + 1] = block
        table[1, i + 1] = jnp.minimum(start // 128, (LENGTH - WIN) // 128)

    local[0].wait()
    remote[0].wait_recv()

    def project(group):
        rows = pl.ds(pl.multiple_of(group * GROUP, GROUP), GROUP)
        place = me.c * 8 + group * 2
        normed = norm_rows(arrived[rows, :].astype(F32), gain_attn[...])
        row = lax.broadcasted_iota(jnp.int32, (128, 128), 0)
        for half in range(2):
            keys = dot(normed, wq[half, 1]).astype(BF16)
            values = dot(normed, wq[half, 2])
            for p in range(2):
                pair, cols = 2 * half + p, slice(p * 128, (p + 1) * 128)
                for b in range(2):
                    kk[pair, place + b] = keys[b * 128 : (b + 1) * 128, cols]
                    vt[pair, place + b, 0:128, :] = values[b * 128 : (b + 1) * 128, cols].T.astype(
                        BF16
                    )
        for half in range(2):
            queries = dot(normed, wq[half, 0]) * QSCALE
            for p in range(2):
                pair, cols = 2 * half + p, slice(p * 128, (p + 1) * 128)
                for b in range(2):
                    turned = queries[b * 128 : (b + 1) * 128, cols].T
                    block = group * 2 + b
                    qt[block, pair, 0:128, 0:128] = jnp.where(row < HDIM, turned, 0.0).astype(BF16)
                    qt[block, pair, 0:128, 128:256] = jnp.where(row >= HDIM, turned, 0.0).astype(
                        BF16
                    )

    def exchange(half, group):
        place = half * 8 + group * 2
        k_part = kk.at[:, pl.ds(place, 2)]
        v_part = vt.at[:, pl.ds(place, 2), pl.ds(0, 128)]
        return [
            pltpu.make_async_remote_copy(
                src_ref=part,
                dst_ref=part,
                send_sem=ss.at[group],
                recv_sem=rs.at[group],
                device_id=me.partner,
                device_id_type=MESH,
            )
            for part, ss, rs in (
                (k_part, ksend_sem, krecv_sem),
                (v_part, vsend_sem, vrecv_sem),
            )
        ]

    for j in (2, 3, 0, 1):
        group = me.group(j)
        relay(
            me, arrived, pl.multiple_of(group * GROUP, GROUP), GROUP,
            rsend_sem.at[group], recv_sem.at[group],
        ).wait_recv()
        project(group)
        for copy in exchange(me.c, group):
            copy.start()
    for j in range(GROUPS):
        for copy in exchange(1 - me.c, me.group(j)):
            copy.wait_recv()

    def score(pair, item, part, dst, top):
        keys = pl.ds(table[1, item] + part * (KEYS // 128), KEYS // 128)
        lhs = jnp.concatenate([kk[pair, keys], marks[keys]], axis=2).reshape(KEYS, 256)
        value = dot(lhs, qt[table[0, item], pair])
        s_refs[dst][part * KEYS : (part + 1) * KEYS, :] = value
        high = jnp.max(value.reshape(KEYS // 8, 8, 256), axis=0)
        return high if top is None else jnp.maximum(top, high)

    def settle(dst, top):
        m_refs[dst][...] = jnp.broadcast_to(jnp.max(top, axis=0, keepdims=True), (8, 256))

    def raise_part(src, part, top):
        rows = slice(part * 128, (part + 1) * 128)
        p_refs[src][rows, :] = jnp.exp2(s_refs[src][rows, :] - top).astype(BF16)

    def weigh(pair, item, src, low, count, total):
        start = table[1, item] + low // 128
        lhs = [vt[pair, start + b] for b in range(count // 128)]
        lhs = jnp.concatenate(lhs, axis=1) if count > 128 else lhs[0]
        value = dot(lhs, p_refs[src][low : low + count, :])
        return value if total is None else total + value

    def conclude(pair, item, total):
        inverse = 1.0 / total[128:129, :]
        result = jnp.concatenate(
            [
                total[0:64, 0:128] * inverse[:, 0:128],
                total[64:128, 128:256] * inverse[:, 128:256],
            ],
            axis=0,
        )
        ctxv[item, :, pair * 128 : (pair + 1) * 128] = result.T.astype(BF16)

    def step(item, pair):
        now, other = pair % 2, 1 - pair % 2
        after, after_pair = (item, pair + 1) if pair < 3 else (item + 1, 0)
        before, before_pair = (item, pair - 1) if pair > 0 else (item - 1, 3)
        top = m_refs[now][0:1, :]
        high = total = None
        for part in range(9):
            if part % 3 == 0:
                high = score(after_pair, after, part // 3, other, high)
            raise_part(now, part, top)
            if part % 2 == 1:
                total = weigh(before_pair, before, other, (part - 1) * 128, 256, total)
        total = weigh(before_pair, before, other, 1024, 128, total)
        conclude(before_pair, before, total)
        settle(other, high)

    def one_item(item, carry):
        for pair in range(4):
            step(item, pair)
        return carry

    table[0, 0] = table[0, 1]
    table[1, 0] = table[1, 1]
    p1[...] = jnp.zeros_like(p1)
    high = None
    for part in range(3):
        high = score(0, 1, part, 0, high)
    settle(0, high)

    def block_context(n):
        begin, first = table[2, n] + 1, table[3, n]
        row = me.c * HALF + in_stream(n, 8) * 128
        nth = patch_of(row + lax.broadcasted_iota(jnp.int32, (128, FEAT), 0)) - first
        value = ctxv[begin]
        for e in range(1, 4):
            value = jnp.where(nth >= e, ctxv[jnp.minimum(begin + e, ITEMS)], value)
        return value

    def finish(j):
        group = in_stream(j, GROUPS)
        low, high = 2 * j + 1 - upward, 2 * j + upward
        ctx = jnp.concatenate([block_context(low), block_context(high)], axis=0)
        rows = pl.ds(pl.multiple_of(group * GROUP, GROUP), GROUP)
        attn = dot(ctx[:, :256], wo[0]) + dot(ctx[:, 256:], wo[1])
        middle = (arrived[rows, :].astype(F32) + attn.astype(BF16).astype(F32)).astype(BF16)
        middle = middle.astype(F32)
        normed = norm_rows(middle, gain_mlp[...])
        result = middle
        for half in range(2):
            hidden = jax.nn.gelu(dot(normed, f1[half]), approximate=True).astype(BF16)
            result = result + dot(hidden, f2[half])
        send[rows, :] = result.astype(BF16)
        send_group(me, group, send, back, me.s, bsend_sem, brecv_sem)

    def stretch(j, carry):
        low = jnp.where(j == 0, 1, 2 * j + 4)
        high = 2 * j + 6
        lax.fori_loop(low, high, one_item, 0)
        total = None
        for part in range(4):
            total = weigh(3, high - 1, 1, part * 256, 256, total)
        conclude(3, high - 1, weigh(3, high - 1, 1, 1024, 128, total))

        @pl.when(j == 0)
        def _():
            await_sends(me, send, arrived, send_sem, recv_sem)
            for i in range(1, 4):
                local[i].wait()
                remote[i].wait_recv()

        finish(j)
        return carry

    lax.fori_loop(0, GROUPS, stretch, 0)

    early = early_groups(me)

    def passing(half, group, recv):
        start = pl.multiple_of(half * HALF + group * GROUP, GROUP)
        return relay(me, back, start, GROUP, rsend_sem.at[group], recv.at[group])

    def hand_on(groups):
        for group in groups:
            passing(me.c, group, brecv_sem).wait_recv()
            passing(me.c, group, rrecv_sem).start()
        for group in groups:
            passing(1 - me.c, group, rrecv_sem).wait_recv()

    hand_on([early, early + 2])

    def place_early(i, carry):
        rows = pl.ds(pl.multiple_of(i * 256, 256), 256)
        column = slot_column(local_slots(rank[:, rows], me.s))
        total = None
        for base in group_bases(early):
            value = dot(picks(column, base), back[pl.ds(base, GROUP), :])
            total = value if total is None else total + value
        placed[rows, :] = total.astype(BF16)
        return carry

    lax.fori_loop(0, LENGTH // 256, place_early, 0)
    outs = [pltpu.make_async_copy(placed, part_ref, out_sem.at[4])]
    outs[0].start()
    hand_on([1 - early, 3 - early])
    for i, base in enumerate(group_bases(1 - early)):
        copy = pltpu.make_async_copy(
            back.at[pl.ds(base, GROUP)], late_ref.at[pl.ds(i * GROUP, GROUP)], out_sem.at[i]
        )
        copy.start()
        outs.append(copy)
    for group in (early, early + 2, 1 - early, 3 - early):
        passing(me.c, group, rrecv_sem).wait_send()
    for copy in outs:
        copy.wait()
    await_sends(me, send, back, bsend_sem, brecv_sem)
    for j in range(GROUPS):
        for copy in exchange(me.c, me.group(j)):
            copy.wait_send()
    for copy in remote:
        copy.wait_send()


def place_kernel(rank, part, late, out):
    me = Place()
    column = slot_column(local_slots(rank[...], me.s))
    total = part[...].astype(F32)
    for i, base in enumerate(group_bases(1 - early_groups(me))):
        total = total + dot(picks(column, base), late[pl.ds(i * GROUP, GROUP), :])
    out[...] = total.astype(BF16)


def body(
    points, curve_rank, patch_counts, norm_gain_attn, w_qkv, w_out, norm_gain_mlp, w_fc1, w_fc2
):
    rank = curve_rank.reshape(1, LENGTH)
    shape = jax.ShapeDtypeStruct
    vm = pl.BlockSpec(memory_space=pltpu.VMEM)
    anywhere = pl.BlockSpec(memory_space=pl.ANY)
    dma = pltpu.SemaphoreType.DMA
    part, late = pl.pallas_call(
        layer_kernel,
        name="layer",
        out_shape=(shape((LENGTH, FEAT), BF16), shape((HALF, FEAT), BF16)),
        in_specs=[vm, vm, pl.BlockSpec(memory_space=pltpu.SMEM), vm, anywhere, anywhere, vm]
        + [anywhere] * 2,
        out_specs=[anywhere] * 2,
        scratch_shapes=[
            VMEM((LENGTH, FEAT), BF16),
            VMEM((LENGTH, FEAT), BF16),
            VMEM((HALF, FEAT), BF16),
            VMEM((HALF, FEAT), BF16),
            VMEM((2,) + w_qkv.shape, BF16),
            VMEM((2,) + w_out.shape, BF16),
            VMEM((2,) + w_fc1.shape, BF16),
            VMEM((2,) + w_fc2.shape, BF16),
            VMEM((4, 16, 128, 128), BF16),
            VMEM((16, 128, 128), BF16),
            VMEM((4, 16, 144, 128), BF16),
            VMEM((8, 4, 256, 256), BF16),
            VMEM((ITEMS + 1, 128, FEAT), BF16),
            VMEM((WIN, 256), F32),
            VMEM((WIN, 256), F32),
            VMEM((WIN, 256), BF16),
            VMEM((WIN, 256), BF16),
            VMEM((8, 256), F32),
            VMEM((8, 256), F32),
            pltpu.SMEM((4, 16), jnp.int32),
            dma, dma((4,)), dma((4,)), dma((4,)), dma((4,)), dma((4,)), dma((4,)),
            dma((4,)), dma((4,)), dma, dma((4,)), dma((4,)), dma((4,)), dma((5,)),
        ],
        compiler_params=pltpu.CompilerParams(collective_id=0, has_side_effects=True),
    )(
        points, rank, patch_counts, norm_gain_attn.reshape(1, FEAT), w_qkv, w_out,
        norm_gain_mlp.reshape(1, FEAT), w_fc1, w_fc2,
    )

    return pl.pallas_call(
        place_kernel,
        name="place_rows",
        grid=(LENGTH // 1024,),
        out_shape=shape((LENGTH, FEAT), BF16),
        in_specs=[
            pl.BlockSpec((1, 1024), lambda i: (0, i)),
            pl.BlockSpec((1024, FEAT), lambda i: (i, 0)),
            pl.BlockSpec((HALF, FEAT), lambda i: (0, 0)),
        ],
        out_specs=pl.BlockSpec((1024, FEAT), lambda i: (i, 0)),
    )(rank, part, late)


def solution(mesh):
    placed = (
        P("space", None),
        P("space"),
        P("space", None),
        P(),
        P(None, None, "mp"),
        P("mp", None),
        P(),
        P(None, "mp"),
        P("mp", None),
    )
    return jax.shard_map(
        body, mesh=mesh, in_specs=placed, out_specs=P("space", None), check_vma=False
    )
```

```python
import functools
import math

import jax
import jax.numpy as jnp
from jax import lax
from jax.experimental import pallas as pl
from jax.experimental.pallas import tpu as pltpu
from jax.sharding import PartitionSpec as P

HDIM = 64
EPS = 1e-06
FAR = -1e30
QSCALE = math.log2(math.e) / math.sqrt(HDIM)

LENGTH = 2048
FEAT = 512
HALF = 1024
SHARDS = 128
PEERS = 64
CELL = 16
GROUP = 256
GROUPS = 4
NX, NZ = 4, 8

MESH = pl.DeviceIdType.MESH
VMEM = pltpu.VMEM
F32 = jnp.float32
BF16 = jnp.bfloat16


def dot(a, b):
    return jnp.dot(a, b, preferred_element_type=F32)


def norm_rows(values, gain):
    average = jnp.mean(values, axis=-1, keepdims=True)
    centred = values - average
    second = jnp.mean(centred * centred, axis=-1, keepdims=True)
    return (centred * lax.rsqrt(second + EPS) * gain).astype(BF16)


class Place:
    def __init__(self):
        self.s = lax.axis_index("space")
        self.c = lax.axis_index("mp")
        self.x = lax.rem(self.s, NX)
        self.z = lax.rem(self.s // NX, NZ)
        self.h = self.s // PEERS
        self.own = self.s - self.h * PEERS
        self.y = self.own // 32
        self.partner = (self.s, 1 - self.c)
        self.has_self = self.h == self.c

    def group(self, j):
        near = self.z // (NZ // 2)
        zh = jnp.where(j < 2, 1 - near, near)
        return lax.rem(self.y + j, 2) * 2 + zh

    def block(self, n):
        return self.group(n // 2) * 2 + n % 2

    def peer(self, first, count, q):
        zz = lax.rem(q // NX + self.z, count // NX)
        xx = lax.rem(q + self.x, NX)
        return first + zz * NX + xx


def greet(me):
    barrier = pltpu.get_barrier_semaphore()

    def one(i, carry):
        peer = lax.rem(me.own + i, PEERS)

        @pl.when(jnp.logical_not(me.has_self & (i == 0)))
        def _():
            pl.semaphore_signal(
                barrier, inc=1, device_id=(me.c * PEERS + peer, me.h), device_id_type=MESH
            )

        return carry

    lax.fori_loop(0, PEERS, one, 0)
    pl.semaphore_signal(barrier, inc=1, device_id=me.partner, device_id_type=MESH)
    return barrier


def await_greetings(me, barrier):
    pl.semaphore_wait(barrier, jnp.where(me.has_self, PEERS, PEERS + 1))


def send_cells(me, first, count, src, dst, at, send_sem, recv_sem):
    landing = pl.multiple_of(at * CELL, CELL)
    mine = me.own // 16

    def one(q, carry):
        peer = me.peer(first, count, q)
        rows = pl.ds(pl.multiple_of(peer * CELL, CELL), CELL)
        itself = me.has_self & (peer == me.own)

        @pl.when(itself)
        def _():
            pltpu.make_async_copy(
                src.at[rows], dst.at[pl.ds(landing, CELL)], recv_sem.at[mine]
            ).start()

        @pl.when(jnp.logical_not(itself))
        def _():
            pltpu.make_async_remote_copy(
                src_ref=src.at[rows],
                dst_ref=dst.at[pl.ds(landing, CELL)],
                send_sem=send_sem,
                recv_sem=recv_sem.at[mine],
                device_id=(me.c * PEERS + peer, me.h),
                device_id_type=MESH,
            ).start()

        return carry

    lax.fori_loop(0, count, one, 0)


def await_sends(me, src, dst, send_sem, recv_sem):
    def over(rows):
        pltpu.make_async_remote_copy(
            src_ref=src.at[pl.ds(0, rows)],
            dst_ref=dst.at[pl.ds(0, rows)],
            send_sem=send_sem,
            recv_sem=recv_sem.at[0],
            device_id=me.partner,
            device_id_type=MESH,
        ).wait_send()

    @pl.when(me.has_self)
    def _():
        over(HALF - CELL)

    @pl.when(jnp.logical_not(me.has_self))
    def _():
        over(HALF)


def relay(me, buf, start, rows, send_sem, recv_sem):
    part = buf.at[pl.ds(start, rows)]
    return pltpu.make_async_remote_copy(
        src_ref=part,
        dst_ref=part,
        send_sem=send_sem,
        recv_sem=recv_sem,
        device_id=me.partner,
        device_id_type=MESH,
    )


def local_slots(rank, s):
    return (rank // LENGTH) * CELL + (rank % LENGTH) - s * CELL


def group_bases(y):
    return [
        pl.multiple_of(half * HALF + (2 * y + k) * GROUP, GROUP)
        for half in range(2)
        for k in range(2)
    ]


def slot_column(slots):
    return jnp.concatenate(
        [
            jnp.broadcast_to(slots[:, p * 128 : (p + 1) * 128], (128, 128)).T
            for p in range(slots.shape[1] // 128)
        ],
        axis=0,
    )


def picks(column, base):
    lane = lax.broadcasted_iota(jnp.int32, column.shape, 1)
    return jnp.concatenate(
        [
            jnp.where(column == lane + (base + t * 128), 1.0, 0.0).astype(BF16)
            for t in range(GROUP // 128)
        ],
        axis=1,
    )


WIN = 1152
KEYS = 384
ITEMS = 11


def layer_kernel(
    points_in, rank_in, counts_in, gain_attn_in, w_qkv, w_out, gain_mlp_in, w_fc1, w_fc2,
    part_ref, late_ref, points, rank, counts, gain_attn, gain_mlp,
    back, placed, send, arrived, wq, wo, f1, f2, kk, marks, vt, qt, ctxv, s0, s1, p0, p1, m0, m1, table,
    send_sem, recv_sem, wloc_sem, wsend_sem, wrecv_sem, ksend_sem, krecv_sem,
    vsend_sem, vrecv_sem, bsend_sem, brecv_sem, rsend_sem, rrecv_sem,
    out_sem, load_sem,
):
    me = Place()
    barrier = greet(me)
    loads = [
        pltpu.make_async_copy(src, dst, load_sem.at[i])
        for i, (src, dst) in enumerate(
            (
                (rank_in, rank),
                (points_in, points),
                (counts_in, counts),
                (gain_attn_in, gain_attn),
                (gain_mlp_in, gain_mlp),
            )
        )
    ]
    for copy in loads:
        copy.start()
    loads[0].wait()
    slots = local_slots(rank[...], me.s)
    s_refs, p_refs, m_refs = (s0, s1), (p0, p1), (m0, m1)

    def permute(group):
        first = me.c * HALF + group * GROUP
        total = jnp.zeros((GROUP, FEAT), F32)
        for part in range(4):
            wanted = first + lax.broadcasted_iota(jnp.int32, (GROUP, 512), 0)
            hit = wanted == slots[:, part * 512 : (part + 1) * 512]
            pick = jnp.where(hit, 1.0, 0.0).astype(BF16)
            total = total + dot(pick, points[pl.ds(part * 512, 512), :])
        send[pl.ds(pl.multiple_of(group * GROUP, GROUP), GROUP), :] = total.astype(BF16)

    local, remote = [], []
    for i, (src, dst) in enumerate(((w_qkv, wq), (w_out, wo), (w_fc1, f1), (w_fc2, f2))):
        copy = pltpu.make_async_copy(src, dst.at[me.c], wloc_sem.at[i])
        copy.start()
        local.append(copy)
        remote.append(
            pltpu.make_async_remote_copy(
                src_ref=src,
                dst_ref=dst.at[me.c],
                send_sem=wsend_sem.at[i],
                recv_sem=wrecv_sem.at[i],
                device_id=me.partner,
                device_id_type=MESH,
            )
        )

    loads[1].wait()
    for j in range(GROUPS):
        group = me.group(j)
        permute(group)
        if j == 0:
            await_greetings(me, barrier)
            remote[0].start()
        send_cells(me, group * 16, 16, send, arrived, me.own, send_sem, recv_sem)
    for copy in remote[1:]:
        copy.start()

    for copy in loads[2:]:
        copy.wait()

    c1 = counts[0, 0]
    c2 = c1 + counts[0, 1]
    c3 = c2 + counts[0, 2]

    def patch_of(position):
        return (
            (position >= c1).astype(jnp.int32)
            + (position >= c2).astype(jnp.int32)
            + (position >= c3).astype(jnp.int32)
        )

    def mark_keys(i, carry):
        patch = patch_of(i * 128 + lax.broadcasted_iota(jnp.int32, (128, 128), 0))
        lane = lax.broadcasted_iota(jnp.int32, (128, 128), 1)
        marks[i] = jnp.where((lane < 4) & (lane != patch), FAR, 0.0).astype(BF16)
        for pair in range(4):
            vt[pair, i, 128:144, :] = jnp.ones((16, 128), BF16)
        return carry

    lax.fori_loop(0, LENGTH // 128, mark_keys, 0)

    def mark_queries(i, carry):
        first = me.c * HALF + i * 128
        patch = patch_of(first + lax.broadcasted_iota(jnp.int32, (128, 256), 1) % 128)
        row = lax.broadcasted_iota(jnp.int32, (128, 256), 0)
        mark = jnp.where(row == patch, 1.0, 0.0).astype(BF16)
        for pair in range(4):
            qt[i, pair, 128:256, :] = mark
        return carry

    lax.fori_loop(0, 8, mark_queries, 0)

    zero = c1 * 0
    firsts, lasts, begins, index = [], [], [], zero
    for n in range(8):
        row = me.c * HALF + me.block(n) * 128
        firsts.append(patch_of(row))
        lasts.append(patch_of(row + 127))
        begins.append(index)
        index = index + lasts[n] - firsts[n] + 1
        table[2, n] = begins[n]
        table[3, n] = firsts[n]
    for i in range(ITEMS + 1):
        block, patch = me.block(0), jnp.minimum(firsts[0] + i, lasts[0])
        for n in range(1, 8):
            reached = begins[n] <= i
            block = jnp.where(reached, me.block(n), block)
            patch = jnp.where(
                reached, jnp.minimum(firsts[n] + i - begins[n], lasts[n]), patch
            )
        start = jnp.where(
            patch >= 3, c3, jnp.where(patch >= 2, c2, jnp.where(patch >= 1, c1, zero))
        )
        table[0, i + 1] = block
        table[1, i + 1] = jnp.minimum(start // 128, (LENGTH - WIN) // 128)

    local[0].wait()
    remote[0].wait_recv()

    def project(group):
        rows = pl.ds(pl.multiple_of(group * GROUP, GROUP), GROUP)
        place = me.c * 8 + group * 2
        normed = norm_rows(arrived[rows, :].astype(F32), gain_attn[...])
        row = lax.broadcasted_iota(jnp.int32, (128, 128), 0)
        for half in range(2):
            keys = dot(normed, wq[half, 1]).astype(BF16)
            values = dot(normed, wq[half, 2])
            for p in range(2):
                pair, cols = 2 * half + p, slice(p * 128, (p + 1) * 128)
                for b in range(2):
                    kk[pair, place + b] = keys[b * 128 : (b + 1) * 128, cols]
                    vt[pair, place + b, 0:128, :] = values[b * 128 : (b + 1) * 128, cols].T.astype(
                        BF16
                    )
        for half in range(2):
            queries = dot(normed, wq[half, 0]) * QSCALE
            for p in range(2):
                pair, cols = 2 * half + p, slice(p * 128, (p + 1) * 128)
                for b in range(2):
                    turned = queries[b * 128 : (b + 1) * 128, cols].T
                    block = group * 2 + b
                    qt[block, pair, 0:128, 0:128] = jnp.where(row < HDIM, turned, 0.0).astype(BF16)
                    qt[block, pair, 0:128, 128:256] = jnp.where(row >= HDIM, turned, 0.0).astype(
                        BF16
                    )

    def exchange(half, group):
        place = half * 8 + group * 2
        k_part = kk.at[:, pl.ds(place, 2)]
        v_part = vt.at[:, pl.ds(place, 2), pl.ds(0, 128)]
        return [
            pltpu.make_async_remote_copy(
                src_ref=part,
                dst_ref=part,
                send_sem=ss.at[group],
                recv_sem=rs.at[group],
                device_id=me.partner,
                device_id_type=MESH,
            )
            for part, ss, rs in (
                (k_part, ksend_sem, krecv_sem),
                (v_part, vsend_sem, vrecv_sem),
            )
        ]

    for j in (0, 2, 3, 1):
        group = me.group(j)
        relay(
            me, arrived, pl.multiple_of(group * GROUP, GROUP), GROUP,
            rsend_sem.at[group], recv_sem.at[group],
        ).wait_recv()
        project(group)
        for copy in exchange(me.c, group):
            copy.start()
    for j in range(GROUPS):
        for copy in exchange(1 - me.c, me.group(j)):
            copy.wait_recv()

    def score(pair, item, part, dst, top):
        keys = pl.ds(table[1, item] + part * (KEYS // 128), KEYS // 128)
        lhs = jnp.concatenate([kk[pair, keys], marks[keys]], axis=2).reshape(KEYS, 256)
        value = dot(lhs, qt[table[0, item], pair])
        s_refs[dst][part * KEYS : (part + 1) * KEYS, :] = value
        high = jnp.max(value.reshape(KEYS // 8, 8, 256), axis=0)
        return high if top is None else jnp.maximum(top, high)

    def settle(dst, top):
        m_refs[dst][...] = jnp.broadcast_to(jnp.max(top, axis=0, keepdims=True), (8, 256))

    def raise_part(src, part, top):
        rows = slice(part * 128, (part + 1) * 128)
        p_refs[src][rows, :] = jnp.exp2(s_refs[src][rows, :] - top).astype(BF16)

    def weigh(pair, item, src, low, count, total):
        start = table[1, item] + low // 128
        lhs = [vt[pair, start + b] for b in range(count // 128)]
        lhs = jnp.concatenate(lhs, axis=1) if count > 128 else lhs[0]
        value = dot(lhs, p_refs[src][low : low + count, :])
        return value if total is None else total + value

    def conclude(pair, item, total):
        inverse = 1.0 / total[128:129, :]
        result = jnp.concatenate(
            [
                total[0:64, 0:128] * inverse[:, 0:128],
                total[64:128, 128:256] * inverse[:, 128:256],
            ],
            axis=0,
        )
        ctxv[item, :, pair * 128 : (pair + 1) * 128] = result.T.astype(BF16)

    def step(item, pair):
        now, other = pair % 2, 1 - pair % 2
        after, after_pair = (item, pair + 1) if pair < 3 else (item + 1, 0)
        before, before_pair = (item, pair - 1) if pair > 0 else (item - 1, 3)
        top = m_refs[now][0:1, :]
        high = total = None
        for part in range(9):
            if part % 3 == 0:
                high = score(after_pair, after, part // 3, other, high)
            raise_part(now, part, top)
            if part % 2 == 1:
                total = weigh(before_pair, before, other, (part - 1) * 128, 256, total)
        total = weigh(before_pair, before, other, 1024, 128, total)
        conclude(before_pair, before, total)
        settle(other, high)

    def one_item(item, carry):
        for pair in range(4):
            step(item, pair)
        return carry

    table[0, 0] = table[0, 1]
    table[1, 0] = table[1, 1]
    p1[...] = jnp.zeros_like(p1)
    high = None
    for part in range(3):
        high = score(0, 1, part, 0, high)
    settle(0, high)

    def block_context(n):
        begin, first = table[2, n] + 1, table[3, n]
        row = me.c * HALF + me.block(n) * 128
        nth = patch_of(row + lax.broadcasted_iota(jnp.int32, (128, FEAT), 0)) - first
        value = ctxv[begin]
        for e in range(1, 4):
            value = jnp.where(nth >= e, ctxv[jnp.minimum(begin + e, ITEMS)], value)
        return value

    def finish(n, blocks):
        ctx = [block_context(n + b) for b in range(blocks)]
        ctx = jnp.concatenate(ctx, axis=0) if blocks > 1 else ctx[0]
        block = me.block(n)
        rows = pl.ds(pl.multiple_of(block * 128, 128), blocks * 128)
        attn = dot(ctx[:, :256], wo[0]) + dot(ctx[:, 256:], wo[1])
        middle = (arrived[rows, :].astype(F32) + attn.astype(BF16).astype(F32)).astype(BF16)
        middle = middle.astype(F32)
        normed = norm_rows(middle, gain_mlp[...])
        result = middle
        for half in range(2):
            hidden = jax.nn.gelu(dot(normed, f1[half]), approximate=True).astype(BF16)
            result = result + dot(hidden, f2[half])
        send[rows, :] = result.astype(BF16)
        send_cells(me, block * 8, blocks * 8, send, back, me.s, bsend_sem, brecv_sem)

    def stretch(k, carry):
        low = jnp.where(k == 0, 1, jnp.where(k == 1, 5, 2 * k + 2))
        high = jnp.where(k == 0, 5, 2 * k + 4)
        lax.fori_loop(low, high, one_item, 0)
        total = None
        for part in range(4):
            total = weigh(3, high - 1, 1, part * 256, 256, total)
        conclude(3, high - 1, weigh(3, high - 1, 1, 1024, 128, total))

        @pl.when(k == 0)
        def _():
            await_sends(me, send, arrived, send_sem, recv_sem)
            for i in range(1, 4):
                local[i].wait()
                remote[i].wait_recv()

        @pl.when(k < 2)
        def _():
            finish(k, 1)

        @pl.when(k >= 2)
        def _():
            finish(2 * k - 2, 2)

        return carry

    lax.fori_loop(0, GROUPS + 1, stretch, 0)

    def passing(half, group, recv):
        start = pl.multiple_of(half * HALF + group * GROUP, GROUP)
        return relay(me, back, start, GROUP, rsend_sem.at[group], recv.at[group])

    def hand_on(groups):
        for group in groups:
            passing(me.c, group, brecv_sem).wait_recv()
            passing(me.c, group, rrecv_sem).start()
        for group in groups:
            passing(1 - me.c, group, rrecv_sem).wait_recv()

    hand_on([me.group(0), me.group(2)])

    def place_early(i, carry):
        rows = pl.ds(pl.multiple_of(i * 256, 256), 256)
        column = slot_column(local_slots(rank[:, rows], me.s))
        total = None
        for base in group_bases(me.y):
            value = dot(picks(column, base), back[pl.ds(base, GROUP), :])
            total = value if total is None else total + value
        placed[rows, :] = total.astype(BF16)
        return carry

    lax.fori_loop(0, LENGTH // 256, place_early, 0)
    outs = [pltpu.make_async_copy(placed, part_ref, out_sem.at[4])]
    outs[0].start()
    hand_on([me.group(3), me.group(1)])
    for i, base in enumerate(group_bases(1 - me.y)):
        copy = pltpu.make_async_copy(
            back.at[pl.ds(base, GROUP)], late_ref.at[pl.ds(i * GROUP, GROUP)], out_sem.at[i]
        )
        copy.start()
        outs.append(copy)
    for group in range(GROUPS):
        passing(me.c, group, rrecv_sem).wait_send()
    for copy in outs:
        copy.wait()
    await_sends(me, send, back, bsend_sem, brecv_sem)
    for j in range(GROUPS):
        for copy in exchange(me.c, me.group(j)):
            copy.wait_send()
    for copy in remote:
        copy.wait_send()


def place_kernel(rank, part, late, out):
    me = Place()
    column = slot_column(local_slots(rank[...], me.s))
    total = part[...].astype(F32)
    for i, base in enumerate(group_bases(1 - me.y)):
        total = total + dot(picks(column, base), late[pl.ds(i * GROUP, GROUP), :])
    out[...] = total.astype(BF16)


def body(
    points, curve_rank, patch_counts, norm_gain_attn, w_qkv, w_out, norm_gain_mlp, w_fc1, w_fc2
):
    rank = curve_rank.reshape(1, LENGTH)
    shape = jax.ShapeDtypeStruct
    vm = pl.BlockSpec(memory_space=pltpu.VMEM)
    anywhere = pl.BlockSpec(memory_space=pl.ANY)
    dma = pltpu.SemaphoreType.DMA
    part, late = pl.pallas_call(
        layer_kernel,
        name="layer",
        out_shape=(shape((LENGTH, FEAT), BF16), shape((HALF, FEAT), BF16)),
        in_specs=[anywhere] * 9,
        out_specs=[anywhere] * 2,
        scratch_shapes=[
            VMEM((LENGTH, FEAT), BF16),
            VMEM((1, LENGTH), jnp.int32),
            pltpu.SMEM((1, 4), jnp.int32),
            VMEM((1, FEAT), F32),
            VMEM((1, FEAT), F32),
            VMEM((LENGTH, FEAT), BF16),
            VMEM((LENGTH, FEAT), BF16),
            VMEM((HALF, FEAT), BF16),
            VMEM((HALF, FEAT), BF16),
            VMEM((2,) + w_qkv.shape, BF16),
            VMEM((2,) + w_out.shape, BF16),
            VMEM((2,) + w_fc1.shape, BF16),
            VMEM((2,) + w_fc2.shape, BF16),
            VMEM((4, 16, 128, 128), BF16),
            VMEM((16, 128, 128), BF16),
            VMEM((4, 16, 144, 128), BF16),
            VMEM((8, 4, 256, 256), BF16),
            VMEM((ITEMS + 1, 128, FEAT), BF16),
            VMEM((WIN, 256), F32),
            VMEM((WIN, 256), F32),
            VMEM((WIN, 256), BF16),
            VMEM((WIN, 256), BF16),
            VMEM((8, 256), F32),
            VMEM((8, 256), F32),
            pltpu.SMEM((4, 16), jnp.int32),
            dma, dma((4,)), dma((4,)), dma((4,)), dma((4,)), dma((4,)), dma((4,)),
            dma((4,)), dma((4,)), dma, dma((4,)), dma((4,)), dma((4,)), dma((5,)), dma((5,)),
        ],
        compiler_params=pltpu.CompilerParams(collective_id=0, has_side_effects=True),
    )(
        points, rank, patch_counts, norm_gain_attn.reshape(1, FEAT), w_qkv, w_out,
        norm_gain_mlp.reshape(1, FEAT), w_fc1, w_fc2,
    )

    return pl.pallas_call(
        place_kernel,
        name="place_rows",
        grid=(LENGTH // 1024,),
        out_shape=shape((LENGTH, FEAT), BF16),
        in_specs=[
            pl.BlockSpec((1, 1024), lambda i: (0, i)),
            pl.BlockSpec((1024, FEAT), lambda i: (i, 0)),
            pl.BlockSpec((HALF, FEAT), lambda i: (0, 0)),
        ],
        out_specs=pl.BlockSpec((1024, FEAT), lambda i: (i, 0)),
    )(rank, part, late)


def solution(mesh):
    placed = (
        P("space", None),
        P("space"),
        P("space", None),
        P(),
        P(None, None, "mp"),
        P("mp", None),
        P(),
        P(None, "mp"),
        P("mp", None),
    )
    return jax.shard_map(
        body, mesh=mesh, in_specs=placed, out_specs=P("space", None), check_vma=False
    )
```

```python
import functools
import math

import jax
import jax.numpy as jnp
from jax import lax
from jax.experimental import pallas as pl
from jax.experimental.pallas import tpu as pltpu
from jax.sharding import PartitionSpec as P

HDIM = 64
EPS = 1e-06
FAR = -1e30
QSCALE = math.log2(math.e) / math.sqrt(HDIM)

LENGTH = 2048
FEAT = 512
HALF = 1024
SHARDS = 128
PEERS = 64
CELL = 16
GROUP = 256
GROUPS = 4
NX, NZ = 4, 8

MESH = pl.DeviceIdType.MESH
VMEM = pltpu.VMEM
F32 = jnp.float32
BF16 = jnp.bfloat16


def dot(a, b):
    return jnp.dot(a, b, preferred_element_type=F32)


def norm_rows(values, gain):
    average = jnp.mean(values, axis=-1, keepdims=True)
    centred = values - average
    second = jnp.mean(centred * centred, axis=-1, keepdims=True)
    return (centred * lax.rsqrt(second + EPS) * gain).astype(BF16)


class Place:
    def __init__(self):
        self.s = lax.axis_index("space")
        self.c = lax.axis_index("mp")
        self.x = lax.rem(self.s, NX)
        self.z = lax.rem(self.s // NX, NZ)
        self.h = self.s // PEERS
        self.own = self.s - self.h * PEERS
        self.y = self.own // 32
        self.partner = (self.s, 1 - self.c)
        self.has_self = self.h == self.c

    def group(self, j):
        near = self.z // (NZ // 2)
        zh = jnp.where(j < 2, 1 - near, near)
        return lax.rem(self.y + j, 2) * 2 + zh

    def block(self, n):
        return self.group(n // 2) * 2 + n % 2

    def peers(self, first, count):
        rows = [lax.rem(self.z + i, count // NX) * NX + first for i in range(count // NX)]
        places = [lax.rem(self.x + i, NX) for i in range(NX)]
        return [rows[q // NX] + places[q % NX] for q in range(count)]


def greet(me):
    barrier = pltpu.get_barrier_semaphore()

    places = [lax.rem(me.x + i, NX) for i in (2, 1, 3, 0)]

    def one(i, carry):
        away = NZ // 2 + (i + 1) // 2 * (2 * lax.rem(i, 2) - 1)
        first = lax.rem(me.z + away, NZ) * NX
        for y in range(2):
            for place in places:
                peer = first + (y * NZ * NX + place)

                @pl.when(jnp.logical_not(me.has_self & (peer == me.own)))
                def _():
                    pl.semaphore_signal(
                        barrier,
                        inc=1,
                        device_id=(me.c * PEERS + peer, me.h),
                        device_id_type=MESH,
                    )

        return carry

    lax.fori_loop(0, NZ, one, 0)
    pl.semaphore_signal(barrier, inc=1, device_id=me.partner, device_id_type=MESH)
    return barrier


def await_greetings(me, barrier):
    pl.semaphore_wait(barrier, jnp.where(me.has_self, PEERS, PEERS + 1))


def send_cells(me, first, count, src, dst, at, send_sem, recv_sem):
    landing = pl.multiple_of(at * CELL, CELL)
    mine = me.own // 16

    for peer in me.peers(first, count):

        @pl.when(jnp.logical_not(me.has_self & (peer == me.own)))
        def _():
            pltpu.make_async_remote_copy(
                src_ref=src.at[pl.ds(pl.multiple_of(peer * CELL, CELL), CELL)],
                dst_ref=dst.at[pl.ds(landing, CELL)],
                send_sem=send_sem,
                recv_sem=recv_sem.at[mine],
                device_id=(me.c * PEERS + peer, me.h),
                device_id_type=MESH,
            ).start()

    @pl.when(me.has_self & (me.own >= first) & (me.own < first + count))
    def _():
        pltpu.make_async_copy(
            src.at[pl.ds(pl.multiple_of(me.own * CELL, CELL), CELL)],
            dst.at[pl.ds(landing, CELL)],
            recv_sem.at[mine],
        ).start()


def await_sends(me, src, dst, send_sem, recv_sem):
    def over(rows):
        pltpu.make_async_remote_copy(
            src_ref=src.at[pl.ds(0, rows)],
            dst_ref=dst.at[pl.ds(0, rows)],
            send_sem=send_sem,
            recv_sem=recv_sem.at[0],
            device_id=me.partner,
            device_id_type=MESH,
        ).wait_send()

    @pl.when(me.has_self)
    def _():
        over(HALF - CELL)

    @pl.when(jnp.logical_not(me.has_self))
    def _():
        over(HALF)


def relay(me, buf, start, rows, send_sem, recv_sem):
    part = buf.at[pl.ds(start, rows)]
    return pltpu.make_async_remote_copy(
        src_ref=part,
        dst_ref=part,
        send_sem=send_sem,
        recv_sem=recv_sem,
        device_id=me.partner,
        device_id_type=MESH,
    )


def local_slots(rank, s):
    return (rank // LENGTH) * CELL + (rank % LENGTH) - s * CELL


def group_bases(y):
    return [
        pl.multiple_of(half * HALF + (2 * y + k) * GROUP, GROUP)
        for half in range(2)
        for k in range(2)
    ]


def slot_column(slots):
    return jnp.concatenate(
        [
            jnp.broadcast_to(slots[:, p * 128 : (p + 1) * 128], (128, 128)).T
            for p in range(slots.shape[1] // 128)
        ],
        axis=0,
    )


def picks(column, base):
    lane = lax.broadcasted_iota(jnp.int32, column.shape, 1)
    return jnp.concatenate(
        [
            jnp.where(column == lane + (base + t * 128), 1.0, 0.0).astype(BF16)
            for t in range(GROUP // 128)
        ],
        axis=1,
    )


WIN = 1152
KEYS = 384
ITEMS = 11


def layer_kernel(
    points_in, rank_in, counts_in, gain_attn_in, w_qkv, w_out, gain_mlp_in, w_fc1, w_fc2,
    part_ref, late_ref, points, rank, counts, gain_attn, gain_mlp,
    back, placed, send, arrived, wq, wo, f1, f2, kk, marks, vt, qt, ctxv, s0, s1, p0, p1, m0, m1, table,
    send_sem, recv_sem, wloc_sem, wsend_sem, wrecv_sem, ksend_sem, krecv_sem,
    vsend_sem, vrecv_sem, bsend_sem, brecv_sem, rsend_sem, rrecv_sem,
    out_sem, load_sem, psend_sem, precv_sem,
):
    me = Place()
    loads = [
        pltpu.make_async_copy(src, dst, load_sem.at[i])
        for i, (src, dst) in enumerate(
            (
                (rank_in, rank),
                (points_in, points),
                (counts_in, counts),
                (gain_attn_in, gain_attn),
                (gain_mlp_in, gain_mlp),
            )
        )
    ]
    for copy in loads:
        copy.start()
    barrier = greet(me)
    loads[0].wait()
    slots = local_slots(rank[...], me.s)
    s_refs, p_refs, m_refs = (s0, s1), (p0, p1), (m0, m1)

    def permute(group):
        first = me.c * HALF + group * GROUP
        total = jnp.zeros((GROUP, FEAT), F32)
        for part in range(4):
            wanted = first + lax.broadcasted_iota(jnp.int32, (GROUP, 512), 0)
            hit = wanted == slots[:, part * 512 : (part + 1) * 512]
            pick = jnp.where(hit, 1.0, 0.0).astype(BF16)
            total = total + dot(pick, points[pl.ds(part * 512, 512), :])
        send[pl.ds(pl.multiple_of(group * GROUP, GROUP), GROUP), :] = total.astype(BF16)

    local, remote = [], []
    for i, (src, dst) in enumerate(((w_qkv, wq), (w_out, wo), (w_fc1, f1), (w_fc2, f2))):
        copy = pltpu.make_async_copy(src, dst.at[me.c], wloc_sem.at[i])
        copy.start()
        local.append(copy)
        remote.append(
            pltpu.make_async_remote_copy(
                src_ref=src,
                dst_ref=dst.at[me.c],
                send_sem=wsend_sem.at[i],
                recv_sem=wrecv_sem.at[i],
                device_id=me.partner,
                device_id_type=MESH,
            )
        )

    loads[1].wait()
    for j in range(GROUPS):
        group = me.group(j)
        permute(group)
        if j == 0:
            await_greetings(me, barrier)
            remote[0].start()
        send_cells(me, group * 16, 16, send, arrived, me.own, send_sem, recv_sem)
    for copy in remote[1:]:
        copy.start()

    for copy in loads[2:]:
        copy.wait()

    c1 = counts[0, 0]
    c2 = c1 + counts[0, 1]
    c3 = c2 + counts[0, 2]

    def patch_of(position):
        return (
            (position >= c1).astype(jnp.int32)
            + (position >= c2).astype(jnp.int32)
            + (position >= c3).astype(jnp.int32)
        )

    def mark_keys(i, carry):
        patch = patch_of(i * 128 + lax.broadcasted_iota(jnp.int32, (128, 128), 0))
        lane = lax.broadcasted_iota(jnp.int32, (128, 128), 1)
        marks[i] = jnp.where((lane < 4) & (lane != patch), FAR, 0.0).astype(BF16)
        for pair in range(4):
            vt[pair, i, 128:144, :] = jnp.ones((16, 128), BF16)
        return carry

    lax.fori_loop(0, LENGTH // 128, mark_keys, 0)

    def mark_queries(i, carry):
        first = me.c * HALF + i * 128
        patch = patch_of(first + lax.broadcasted_iota(jnp.int32, (128, 256), 1) % 128)
        row = lax.broadcasted_iota(jnp.int32, (128, 256), 0)
        mark = jnp.where(row == patch, 1.0, 0.0).astype(BF16)
        for pair in range(4):
            qt[i, pair, 128:256, :] = mark
        return carry

    lax.fori_loop(0, 8, mark_queries, 0)

    zero = c1 * 0
    firsts, lasts, begins, index = [], [], [], zero
    for n in range(8):
        row = me.c * HALF + me.block(n) * 128
        firsts.append(patch_of(row))
        lasts.append(patch_of(row + 127))
        begins.append(index)
        index = index + lasts[n] - firsts[n] + 1
        table[2, n] = begins[n]
        table[3, n] = firsts[n]
    for i in range(ITEMS + 1):
        block, patch = me.block(0), jnp.minimum(firsts[0] + i, lasts[0])
        for n in range(1, 8):
            reached = begins[n] <= i
            block = jnp.where(reached, me.block(n), block)
            patch = jnp.where(
                reached, jnp.minimum(firsts[n] + i - begins[n], lasts[n]), patch
            )
        start = jnp.where(
            patch >= 3, c3, jnp.where(patch >= 2, c2, jnp.where(patch >= 1, c1, zero))
        )
        table[0, i + 1] = block
        table[1, i + 1] = jnp.minimum(start // 128, (LENGTH - WIN) // 128)

    local[0].wait()
    remote[0].wait_recv()

    def project(group):
        rows = pl.ds(pl.multiple_of(group * GROUP, GROUP), GROUP)
        place = me.c * 8 + group * 2
        normed = norm_rows(arrived[rows, :].astype(F32), gain_attn[...])
        row = lax.broadcasted_iota(jnp.int32, (128, 128), 0)
        for half in range(2):
            keys = dot(normed, wq[half, 1]).astype(BF16)
            values = dot(normed, wq[half, 2])
            for p in range(2):
                pair, cols = 2 * half + p, slice(p * 128, (p + 1) * 128)
                for b in range(2):
                    kk[pair, place + b] = keys[b * 128 : (b + 1) * 128, cols]
                    vt[pair, place + b, 0:128, :] = values[b * 128 : (b + 1) * 128, cols].T.astype(
                        BF16
                    )
        for half in range(2):
            queries = dot(normed, wq[half, 0]) * QSCALE
            for p in range(2):
                pair, cols = 2 * half + p, slice(p * 128, (p + 1) * 128)
                for b in range(2):
                    turned = queries[b * 128 : (b + 1) * 128, cols].T
                    block = group * 2 + b
                    qt[block, pair, 0:128, 0:128] = jnp.where(row < HDIM, turned, 0.0).astype(BF16)
                    qt[block, pair, 0:128, 128:256] = jnp.where(row >= HDIM, turned, 0.0).astype(
                        BF16
                    )

    def exchange(half, group):
        place = half * 8 + group * 2
        k_part = kk.at[:, pl.ds(place, 2)]
        v_part = vt.at[:, pl.ds(place, 2), pl.ds(0, 128)]
        return [
            pltpu.make_async_remote_copy(
                src_ref=part,
                dst_ref=part,
                send_sem=ss.at[group],
                recv_sem=rs.at[group],
                device_id=me.partner,
                device_id_type=MESH,
            )
            for part, ss, rs in (
                (k_part, ksend_sem, krecv_sem),
                (v_part, vsend_sem, vrecv_sem),
            )
        ]

    for j in (0, 2, 3, 1):
        group = me.group(j)
        relay(
            me, arrived, pl.multiple_of(group * GROUP, GROUP), GROUP,
            rsend_sem.at[group], recv_sem.at[group],
        ).wait_recv()
        project(group)
        for copy in exchange(me.c, group):
            copy.start()
    for j in range(GROUPS):
        for copy in exchange(1 - me.c, me.group(j)):
            copy.wait_recv()

    def score(pair, item, part, dst, top):
        keys = pl.ds(table[1, item] + part * (KEYS // 128), KEYS // 128)
        lhs = jnp.concatenate([kk[pair, keys], marks[keys]], axis=2).reshape(KEYS, 256)
        value = dot(lhs, qt[table[0, item], pair])
        s_refs[dst][part * KEYS : (part + 1) * KEYS, :] = value
        high = jnp.max(value.reshape(KEYS // 8, 8, 256), axis=0)
        return high if top is None else jnp.maximum(top, high)

    def settle(dst, top):
        m_refs[dst][...] = jnp.broadcast_to(jnp.max(top, axis=0, keepdims=True), (8, 256))

    def raise_part(src, part, top):
        rows = slice(part * 128, (part + 1) * 128)
        p_refs[src][rows, :] = jnp.exp2(s_refs[src][rows, :] - top).astype(BF16)

    def weigh(pair, item, src, low, count, total):
        start = table[1, item] + low // 128
        lhs = [vt[pair, start + b] for b in range(count // 128)]
        lhs = jnp.concatenate(lhs, axis=1) if count > 128 else lhs[0]
        value = dot(lhs, p_refs[src][low : low + count, :])
        return value if total is None else total + value

    def conclude(pair, item, total):
        inverse = 1.0 / total[128:129, :]
        result = jnp.concatenate(
            [
                total[0:64, 0:128] * inverse[:, 0:128],
                total[64:128, 128:256] * inverse[:, 128:256],
            ],
            axis=0,
        )
        ctxv[item, :, pair * 128 : (pair + 1) * 128] = result.T.astype(BF16)

    def step(item, pair):
        now, other = pair % 2, 1 - pair % 2
        after, after_pair = (item, pair + 1) if pair < 3 else (item + 1, 0)
        before, before_pair = (item, pair - 1) if pair > 0 else (item - 1, 3)
        top = m_refs[now][0:1, :]
        high = total = None
        for part in range(9):
            if part % 3 == 0:
                high = score(after_pair, after, part // 3, other, high)
            raise_part(now, part, top)
            if part % 2 == 1:
                total = weigh(before_pair, before, other, (part - 1) * 128, 256, total)
        total = weigh(before_pair, before, other, 1024, 128, total)
        conclude(before_pair, before, total)
        settle(other, high)

    def one_item(item, carry):
        for pair in range(4):
            step(item, pair)
        return carry

    table[0, 0] = table[0, 1]
    table[1, 0] = table[1, 1]
    p1[...] = jnp.zeros_like(p1)
    high = None
    for part in range(3):
        high = score(0, 1, part, 0, high)
    settle(0, high)

    def block_context(n):
        begin, first = table[2, n] + 1, table[3, n]
        row = me.c * HALF + me.block(n) * 128
        nth = patch_of(row + lax.broadcasted_iota(jnp.int32, (128, FEAT), 0)) - first
        value = ctxv[begin]
        for e in range(1, 4):
            value = jnp.where(nth >= e, ctxv[jnp.minimum(begin + e, ITEMS)], value)
        return value

    def finish(n, blocks):
        ctx = [block_context(n + b) for b in range(blocks)]
        ctx = jnp.concatenate(ctx, axis=0) if blocks > 1 else ctx[0]
        block = me.block(n)
        rows = pl.ds(pl.multiple_of(block * 128, 128), blocks * 128)
        attn = dot(ctx[:, :256], wo[0]) + dot(ctx[:, 256:], wo[1])
        middle = (arrived[rows, :].astype(F32) + attn.astype(BF16).astype(F32)).astype(BF16)
        middle = middle.astype(F32)
        normed = norm_rows(middle, gain_mlp[...])
        result = middle
        for half in range(2):
            hidden = jax.nn.gelu(dot(normed, f1[half]), approximate=True).astype(BF16)
            result = result + dot(hidden, f2[half])
        send[rows, :] = result.astype(BF16)
        send_cells(me, block * 8, blocks * 8, send, back, me.s, bsend_sem, brecv_sem)

    def stretch(k, carry):
        low = jnp.where(k == 0, 1, jnp.where(k == 1, 5, 2 * k + 2))
        high = jnp.where(k == 0, 5, 2 * k + 4)
        lax.fori_loop(low, high, one_item, 0)
        total = None
        for part in range(4):
            total = weigh(3, high - 1, 1, part * 256, 256, total)
        conclude(3, high - 1, weigh(3, high - 1, 1, 1024, 128, total))

        @pl.when(k == 0)
        def _():
            await_sends(me, send, arrived, send_sem, recv_sem)
            for i in range(1, 4):
                local[i].wait()
                remote[i].wait_recv()

        @pl.when(k < 2)
        def _():
            finish(k, 1)

        @pl.when(k >= 2)
        def _():
            finish(2 * k - 2, 2)

        return carry

    lax.fori_loop(0, GROUPS + 1, stretch, 0)

    def passing(half, group, recv):
        start = pl.multiple_of(half * HALF + group * GROUP, GROUP)
        return relay(me, back, start, GROUP, rsend_sem.at[group], recv.at[group])

    def hand_on(groups, awaited):
        for group in groups:
            passing(me.c, group, brecv_sem).wait_recv()
            passing(me.c, group, rrecv_sem).start()
        for group in awaited:
            passing(1 - me.c, group, rrecv_sem).wait_recv()

    def place_early(i, carry):
        start = pl.multiple_of(me.c * HALF + i * 256, 256)
        column = slot_column(local_slots(rank[:, pl.ds(start, 256)], me.s))
        total = None
        for base in group_bases(me.y):
            value = dot(picks(column, base), back[pl.ds(base, GROUP), :])
            total = value if total is None else total + value
        placed[pl.ds(start, 256), :] = total.astype(BF16)
        return carry

    def placed_half(half):
        start = pl.multiple_of(half * HALF, HALF)
        rows = pl.ds(start, HALF)
        return (
            relay(me, placed, start, HALF, psend_sem, precv_sem),
            pltpu.make_async_copy(placed.at[rows], part_ref.at[rows], out_sem.at[4 + half]),
        )

    hand_on([me.group(0), me.group(2)], [me.group(0), me.group(2)])
    lax.fori_loop(0, HALF // 256, place_early, 0)
    to_partner, own_out = placed_half(me.c)
    from_partner, partner_out = placed_half(1 - me.c)
    to_partner.start()
    own_out.start()
    hand_on([me.group(3)], [])
    from_partner.wait_recv()
    partner_out.start()
    hand_on([me.group(1)], [me.group(3), me.group(1)])
    outs = [own_out, partner_out]
    for i, base in enumerate(group_bases(1 - me.y)):
        copy = pltpu.make_async_copy(
            back.at[pl.ds(base, GROUP)], late_ref.at[pl.ds(i * GROUP, GROUP)], out_sem.at[i]
        )
        copy.start()
        outs.append(copy)
    to_partner.wait_send()
    for group in range(GROUPS):
        passing(me.c, group, rrecv_sem).wait_send()
    for copy in outs:
        copy.wait()
    await_sends(me, send, back, bsend_sem, brecv_sem)
    for j in range(GROUPS):
        for copy in exchange(me.c, me.group(j)):
            copy.wait_send()
    for copy in remote:
        copy.wait_send()


def place_kernel(rank, part, late, out):
    me = Place()
    column = slot_column(local_slots(rank[...], me.s))
    total = part[...].astype(F32)
    for i, base in enumerate(group_bases(1 - me.y)):
        total = total + dot(picks(column, base), late[pl.ds(i * GROUP, GROUP), :])
    out[...] = total.astype(BF16)


def body(
    points, curve_rank, patch_counts, norm_gain_attn, w_qkv, w_out, norm_gain_mlp, w_fc1, w_fc2
):
    rank = curve_rank.reshape(1, LENGTH)
    shape = jax.ShapeDtypeStruct
    vm = pl.BlockSpec(memory_space=pltpu.VMEM)
    anywhere = pl.BlockSpec(memory_space=pl.ANY)
    dma = pltpu.SemaphoreType.DMA
    part, late = pl.pallas_call(
        layer_kernel,
        name="layer",
        out_shape=(shape((LENGTH, FEAT), BF16), shape((HALF, FEAT), BF16)),
        in_specs=[anywhere] * 9,
        out_specs=[anywhere] * 2,
        scratch_shapes=[
            VMEM((LENGTH, FEAT), BF16),
            VMEM((1, LENGTH), jnp.int32),
            pltpu.SMEM((1, 4), jnp.int32),
            VMEM((1, FEAT), F32),
            VMEM((1, FEAT), F32),
            VMEM((LENGTH, FEAT), BF16),
            VMEM((LENGTH, FEAT), BF16),
            VMEM((HALF, FEAT), BF16),
            VMEM((HALF, FEAT), BF16),
            VMEM((2,) + w_qkv.shape, BF16),
            VMEM((2,) + w_out.shape, BF16),
            VMEM((2,) + w_fc1.shape, BF16),
            VMEM((2,) + w_fc2.shape, BF16),
            VMEM((4, 16, 128, 128), BF16),
            VMEM((16, 128, 128), BF16),
            VMEM((4, 16, 144, 128), BF16),
            VMEM((8, 4, 256, 256), BF16),
            VMEM((ITEMS + 1, 128, FEAT), BF16),
            VMEM((WIN, 256), F32),
            VMEM((WIN, 256), F32),
            VMEM((WIN, 256), BF16),
            VMEM((WIN, 256), BF16),
            VMEM((8, 256), F32),
            VMEM((8, 256), F32),
            pltpu.SMEM((4, 16), jnp.int32),
            dma, dma((4,)), dma((4,)), dma((4,)), dma((4,)), dma((4,)), dma((4,)),
            dma((4,)), dma((4,)), dma, dma((4,)), dma((4,)), dma((4,)), dma((6,)), dma((5,)), dma, dma,
        ],
        compiler_params=pltpu.CompilerParams(collective_id=0, has_side_effects=True),
    )(
        points, rank, patch_counts, norm_gain_attn.reshape(1, FEAT), w_qkv, w_out,
        norm_gain_mlp.reshape(1, FEAT), w_fc1, w_fc2,
    )

    return pl.pallas_call(
        place_kernel,
        name="place_rows",
        grid=(LENGTH // 1024,),
        out_shape=shape((LENGTH, FEAT), BF16),
        in_specs=[
            pl.BlockSpec((1, 1024), lambda i: (0, i)),
            pl.BlockSpec((1024, FEAT), lambda i: (i, 0)),
            pl.BlockSpec((HALF, FEAT), lambda i: (0, 0)),
        ],
        out_specs=pl.BlockSpec((1024, FEAT), lambda i: (i, 0)),
    )(rank, part, late)


def solution(mesh):
    placed = (
        P("space", None),
        P("space"),
        P("space", None),
        P(),
        P(None, None, "mp"),
        P("mp", None),
        P(),
        P(None, "mp"),
        P("mp", None),
    )
    return jax.shard_map(
        body, mesh=mesh, in_specs=placed, out_specs=P("space", None), check_vma=False
    )
```

```python
import functools
import math

import jax
import jax.numpy as jnp
from jax import lax
from jax.experimental import pallas as pl
from jax.experimental.pallas import tpu as pltpu
from jax.sharding import PartitionSpec as P

HDIM = 64
EPS = 1e-06
FAR = -1e30
QSCALE = math.log2(math.e) / math.sqrt(HDIM)

LENGTH = 2048
FEAT = 512
HALF = 1024
SHARDS = 128
PEERS = 64
CELL = 16
GROUP = 256
GROUPS = 4
NX, NZ = 4, 8

MESH = pl.DeviceIdType.MESH
VMEM = pltpu.VMEM
F32 = jnp.float32
BF16 = jnp.bfloat16


def dot(a, b):
    return jnp.dot(a, b, preferred_element_type=F32)


def norm_rows(values, gain):
    average = jnp.mean(values, axis=-1, keepdims=True)
    centred = values - average
    second = jnp.mean(centred * centred, axis=-1, keepdims=True)
    return (centred * lax.rsqrt(second + EPS) * gain).astype(BF16)


def twice_gelu(x):
    scale = math.sqrt(2.0 / math.pi)
    inner = x * (scale + (scale * 0.044715) * (x * x))
    return (x * (1.0 + jnp.tanh(inner))).astype(BF16)


class Place:
    def __init__(self):
        self.s = lax.axis_index("space")
        self.c = lax.axis_index("mp")
        self.x = lax.rem(self.s, NX)
        self.z = lax.rem(self.s // NX, NZ)
        self.h = self.s // PEERS
        self.own = self.s - self.h * PEERS
        self.y = self.own // 32
        self.partner = (self.s, 1 - self.c)
        self.has_self = self.h == self.c

    def group(self, j):
        near = self.z // (NZ // 2)
        zh = jnp.where(j < 2, 1 - near, near)
        return lax.rem(self.y + j, 2) * 2 + zh

    def block(self, n):
        return self.group(n // 2) * 2 + n % 2

    def peers(self, first, count):
        rows = [lax.rem(self.z + i, count // NX) * NX + first for i in range(count // NX)]
        places = [lax.rem(self.x + i, NX) for i in range(NX)]
        return [rows[q // NX] + places[q % NX] for q in range(count)]


def greet(me):
    barrier = pltpu.get_barrier_semaphore()

    places = [lax.rem(me.x + i, NX) for i in (2, 1, 3, 0)]

    def one(i, carry):
        away = NZ // 2 + (i + 1) // 2 * (2 * lax.rem(i, 2) - 1)
        first = lax.rem(me.z + away, NZ) * NX
        for y in range(2):
            for place in places:
                peer = first + (y * NZ * NX + place)

                @pl.when(jnp.logical_not(me.has_self & (peer == me.own)))
                def _():
                    pl.semaphore_signal(
                        barrier,
                        inc=1,
                        device_id=(me.c * PEERS + peer, me.h),
                        device_id_type=MESH,
                    )

        return carry

    lax.fori_loop(0, NZ, one, 0)
    pl.semaphore_signal(barrier, inc=1, device_id=me.partner, device_id_type=MESH)
    return barrier


def await_greetings(me, barrier):
    pl.semaphore_wait(barrier, jnp.where(me.has_self, PEERS, PEERS + 1))


def send_cells(me, first, count, src, dst, at, send_sem, recv_sem):
    landing = pl.multiple_of(at * CELL, CELL)
    mine = me.own // 16

    for peer in me.peers(first, count):

        @pl.when(jnp.logical_not(me.has_self & (peer == me.own)))
        def _():
            pltpu.make_async_remote_copy(
                src_ref=src.at[pl.ds(pl.multiple_of(peer * CELL, CELL), CELL)],
                dst_ref=dst.at[pl.ds(landing, CELL)],
                send_sem=send_sem,
                recv_sem=recv_sem.at[mine],
                device_id=(me.c * PEERS + peer, me.h),
                device_id_type=MESH,
            ).start()

    @pl.when(me.has_self & (me.own >= first) & (me.own < first + count))
    def _():
        pltpu.make_async_copy(
            src.at[pl.ds(pl.multiple_of(me.own * CELL, CELL), CELL)],
            dst.at[pl.ds(landing, CELL)],
            recv_sem.at[mine],
        ).start()


def await_sends(me, src, dst, send_sem, recv_sem):
    def over(rows):
        pltpu.make_async_remote_copy(
            src_ref=src.at[pl.ds(0, rows)],
            dst_ref=dst.at[pl.ds(0, rows)],
            send_sem=send_sem,
            recv_sem=recv_sem.at[0],
            device_id=me.partner,
            device_id_type=MESH,
        ).wait_send()

    @pl.when(me.has_self)
    def _():
        over(HALF - CELL)

    @pl.when(jnp.logical_not(me.has_self))
    def _():
        over(HALF)


def relay(me, buf, start, rows, send_sem, recv_sem):
    part = buf.at[pl.ds(start, rows)]
    return pltpu.make_async_remote_copy(
        src_ref=part,
        dst_ref=part,
        send_sem=send_sem,
        recv_sem=recv_sem,
        device_id=me.partner,
        device_id_type=MESH,
    )


def local_slots(rank, s):
    return (rank // LENGTH) * CELL + (rank % LENGTH) - s * CELL


def group_bases(y):
    return [
        pl.multiple_of(half * HALF + (2 * y + k) * GROUP, GROUP)
        for half in range(2)
        for k in range(2)
    ]


def slot_column(slots):
    return jnp.concatenate(
        [
            jnp.broadcast_to(slots[:, p * 128 : (p + 1) * 128], (128, 128)).T
            for p in range(slots.shape[1] // 128)
        ],
        axis=0,
    )


def picks(column, base):
    lane = lax.broadcasted_iota(jnp.int32, column.shape, 1)
    return jnp.concatenate(
        [
            jnp.where(column == lane + (base + t * 128), 1.0, 0.0).astype(BF16)
            for t in range(GROUP // 128)
        ],
        axis=1,
    )


WIN = 1152
KEYS = 384
ITEMS = 11


def layer_kernel(
    points_in, rank_in, counts_in, gain_attn_in, w_qkv, w_out, gain_mlp_in, w_fc1, w_fc2,
    part_ref, late_ref, points, rank, counts, gain_attn, gain_mlp,
    back, placed, send, arrived, wq, wo, f1, f2, kk, marks, vt, qt, ctxv, s0, s1, p0, p1, m0, m1, table,
    send_sem, recv_sem, wloc_sem, wsend_sem, wrecv_sem, ksend_sem, krecv_sem,
    vsend_sem, vrecv_sem, bsend_sem, brecv_sem, rsend_sem, rrecv_sem,
    out_sem, load_sem, psend_sem, precv_sem,
):
    me = Place()
    loads = [
        pltpu.make_async_copy(src, dst, load_sem.at[i])
        for i, (src, dst) in enumerate(
            (
                (rank_in, rank),
                (points_in, points),
                (counts_in, counts),
                (gain_attn_in, gain_attn),
                (gain_mlp_in, gain_mlp),
            )
        )
    ]
    for copy in loads:
        copy.start()
    barrier = greet(me)
    loads[0].wait()
    slots = local_slots(rank[...], me.s)
    s_refs, p_refs, m_refs = (s0, s1), (p0, p1), (m0, m1)

    def permute(group):
        first = me.c * HALF + group * GROUP
        total = jnp.zeros((GROUP, FEAT), F32)
        for part in range(4):
            wanted = first + lax.broadcasted_iota(jnp.int32, (GROUP, 512), 0)
            hit = wanted == slots[:, part * 512 : (part + 1) * 512]
            pick = jnp.where(hit, 1.0, 0.0).astype(BF16)
            total = total + dot(pick, points[pl.ds(part * 512, 512), :])
        send[pl.ds(pl.multiple_of(group * GROUP, GROUP), GROUP), :] = total.astype(BF16)

    local, remote = [], []
    for i, (src, dst) in enumerate(((w_qkv, wq), (w_out, wo), (w_fc1, f1), (w_fc2, f2))):
        copy = pltpu.make_async_copy(src, dst.at[me.c], wloc_sem.at[i])
        copy.start()
        local.append(copy)
        remote.append(
            pltpu.make_async_remote_copy(
                src_ref=src,
                dst_ref=dst.at[me.c],
                send_sem=wsend_sem.at[i],
                recv_sem=wrecv_sem.at[i],
                device_id=me.partner,
                device_id_type=MESH,
            )
        )

    loads[1].wait()
    for j in range(GROUPS):
        group = me.group(j)
        permute(group)
        if j == 0:
            await_greetings(me, barrier)
            remote[0].start()
        send_cells(me, group * 16, 16, send, arrived, me.own, send_sem, recv_sem)
    for copy in remote[1:]:
        copy.start()

    for copy in loads[2:]:
        copy.wait()

    c1 = counts[0, 0]
    c2 = c1 + counts[0, 1]
    c3 = c2 + counts[0, 2]

    def patch_of(position):
        return (
            (position >= c1).astype(jnp.int32)
            + (position >= c2).astype(jnp.int32)
            + (position >= c3).astype(jnp.int32)
        )

    def mark_keys(i, carry):
        patch = patch_of(i * 128 + lax.broadcasted_iota(jnp.int32, (128, 128), 0))
        lane = lax.broadcasted_iota(jnp.int32, (128, 128), 1)
        marks[i] = jnp.where((lane < 4) & (lane != patch), FAR, 0.0).astype(BF16)
        for pair in range(4):
            vt[pair, i, 128:144, :] = jnp.ones((16, 128), BF16)
        return carry

    lax.fori_loop(0, LENGTH // 128, mark_keys, 0)

    def mark_queries(i, carry):
        first = me.c * HALF + i * 128
        patch = patch_of(first + lax.broadcasted_iota(jnp.int32, (128, 256), 1) % 128)
        row = lax.broadcasted_iota(jnp.int32, (128, 256), 0)
        mark = jnp.where(row == patch, 1.0, 0.0).astype(BF16)
        for pair in range(4):
            qt[i, pair, 128:256, :] = mark
        return carry

    lax.fori_loop(0, 8, mark_queries, 0)

    zero = c1 * 0
    firsts, lasts, begins, index = [], [], [], zero
    for n in range(8):
        row = me.c * HALF + me.block(n) * 128
        firsts.append(patch_of(row))
        lasts.append(patch_of(row + 127))
        begins.append(index)
        index = index + lasts[n] - firsts[n] + 1
        table[2, n] = begins[n]
        table[3, n] = firsts[n]
    for i in range(ITEMS + 1):
        block, patch = me.block(0), jnp.minimum(firsts[0] + i, lasts[0])
        for n in range(1, 8):
            reached = begins[n] <= i
            block = jnp.where(reached, me.block(n), block)
            patch = jnp.where(
                reached, jnp.minimum(firsts[n] + i - begins[n], lasts[n]), patch
            )
        start = jnp.where(
            patch >= 3, c3, jnp.where(patch >= 2, c2, jnp.where(patch >= 1, c1, zero))
        )
        table[0, i + 1] = block
        table[1, i + 1] = jnp.minimum(start // 128, (LENGTH - WIN) // 128)

    local[0].wait()
    remote[0].wait_recv()

    def project(group):
        rows = pl.ds(pl.multiple_of(group * GROUP, GROUP), GROUP)
        place = me.c * 8 + group * 2
        normed = norm_rows(arrived[rows, :].astype(F32), gain_attn[...])
        row = lax.broadcasted_iota(jnp.int32, (128, 128), 0)
        for half in range(2):
            keys = dot(normed, wq[half, 1]).astype(BF16)
            values = dot(normed, wq[half, 2])
            for p in range(2):
                pair, cols = 2 * half + p, slice(p * 128, (p + 1) * 128)
                for b in range(2):
                    kk[pair, place + b] = keys[b * 128 : (b + 1) * 128, cols]
                    vt[pair, place + b, 0:128, :] = values[b * 128 : (b + 1) * 128, cols].T.astype(
                        BF16
                    )
        for half in range(2):
            queries = dot(normed, wq[half, 0]) * QSCALE
            for p in range(2):
                pair, cols = 2 * half + p, slice(p * 128, (p + 1) * 128)
                for b in range(2):
                    turned = queries[b * 128 : (b + 1) * 128, cols].T
                    block = group * 2 + b
                    qt[block, pair, 0:128, 0:128] = jnp.where(row < HDIM, turned, 0.0).astype(BF16)
                    qt[block, pair, 0:128, 128:256] = jnp.where(row >= HDIM, turned, 0.0).astype(
                        BF16
                    )

    def exchange(half, group):
        place = half * 8 + group * 2
        k_part = kk.at[:, pl.ds(place, 2)]
        v_part = vt.at[:, pl.ds(place, 2), pl.ds(0, 128)]
        return [
            pltpu.make_async_remote_copy(
                src_ref=part,
                dst_ref=part,
                send_sem=ss.at[group],
                recv_sem=rs.at[group],
                device_id=me.partner,
                device_id_type=MESH,
            )
            for part, ss, rs in (
                (k_part, ksend_sem, krecv_sem),
                (v_part, vsend_sem, vrecv_sem),
            )
        ]

    for j in (0, 2, 3, 1):
        group = me.group(j)
        relay(
            me, arrived, pl.multiple_of(group * GROUP, GROUP), GROUP,
            rsend_sem.at[group], recv_sem.at[group],
        ).wait_recv()
        project(group)
        for copy in exchange(me.c, group):
            copy.start()
    for j in range(GROUPS):
        for copy in exchange(1 - me.c, me.group(j)):
            copy.wait_recv()

    def score(pair, item, part, dst, top):
        keys = pl.ds(table[1, item] + part * (KEYS // 128), KEYS // 128)
        lhs = jnp.concatenate([kk[pair, keys], marks[keys]], axis=2).reshape(KEYS, 256)
        value = dot(lhs, qt[table[0, item], pair])
        s_refs[dst][part * KEYS : (part + 1) * KEYS, :] = value
        high = jnp.max(value.reshape(KEYS // 8, 8, 256), axis=0)
        return high if top is None else jnp.maximum(top, high)

    def settle(dst, top):
        m_refs[dst][...] = jnp.broadcast_to(jnp.max(top, axis=0, keepdims=True), (8, 256))

    def raise_part(src, part, top):
        rows = slice(part * 128, (part + 1) * 128)
        p_refs[src][rows, :] = jnp.exp2(s_refs[src][rows, :] - top).astype(BF16)

    def weigh(pair, item, src, low, count, total):
        start = table[1, item] + low // 128
        lhs = [vt[pair, start + b] for b in range(count // 128)]
        lhs = jnp.concatenate(lhs, axis=1) if count > 128 else lhs[0]
        value = dot(lhs, p_refs[src][low : low + count, :])
        return value if total is None else total + value

    def conclude(pair, item, total):
        inverse = 1.0 / total[128:129, :]
        result = jnp.concatenate(
            [
                total[0:64, 0:128] * inverse[:, 0:128],
                total[64:128, 128:256] * inverse[:, 128:256],
            ],
            axis=0,
        )
        ctxv[item, :, pair * 128 : (pair + 1) * 128] = result.T.astype(BF16)

    def step(item, pair):
        now, other = pair % 2, 1 - pair % 2
        after, after_pair = (item, pair + 1) if pair < 3 else (item + 1, 0)
        before, before_pair = (item, pair - 1) if pair > 0 else (item - 1, 3)
        top = m_refs[now][0:1, :]
        high = total = None
        for part in range(9):
            if part % 3 == 0:
                high = score(after_pair, after, part // 3, other, high)
            raise_part(now, part, top)
            if part % 2 == 1:
                total = weigh(before_pair, before, other, (part - 1) * 128, 256, total)
        total = weigh(before_pair, before, other, 1024, 128, total)
        conclude(before_pair, before, total)
        settle(other, high)

    def one_item(item, carry):
        for pair in range(4):
            step(item, pair)
        return carry

    table[0, 0] = table[0, 1]
    table[1, 0] = table[1, 1]
    p1[...] = jnp.zeros_like(p1)
    high = None
    for part in range(3):
        high = score(0, 1, part, 0, high)
    settle(0, high)

    def block_context(n):
        begin, first = table[2, n] + 1, table[3, n]
        row = me.c * HALF + me.block(n) * 128
        place = lax.broadcasted_iota(jnp.int32, (128, FEAT), 0)
        value = ctxv[begin]
        for e in range(1, 4):
            patch = first + e
            start = jnp.where(
                patch == 1, c1, jnp.where(patch == 2, c2, jnp.where(patch == 3, c3, LENGTH))
            )
            other = ctxv[jnp.minimum(begin + e, ITEMS)]
            value = jnp.where(place >= start - row, other, value)
        return value

    def finish(n, blocks):
        ctx = [block_context(n + b) for b in range(blocks)]
        ctx = jnp.concatenate(ctx, axis=0) if blocks > 1 else ctx[0]
        block = me.block(n)
        rows = pl.ds(pl.multiple_of(block * 128, 128), blocks * 128)
        attn = dot(ctx[:, :256], wo[0]) + dot(ctx[:, 256:], wo[1])
        middle = (arrived[rows, :].astype(F32) + attn.astype(BF16).astype(F32)).astype(BF16)
        middle = middle.astype(F32)
        normed = norm_rows(middle, gain_mlp[...])
        total = None
        for half in range(2):
            value = dot(twice_gelu(dot(normed, f1[half])), f2[half])
            total = value if total is None else total + value
        send[rows, :] = (middle + 0.5 * total).astype(BF16)
        send_cells(me, block * 8, blocks * 8, send, back, me.s, bsend_sem, brecv_sem)

    def stretch(k, carry):
        low = jnp.where(k == 0, 1, jnp.where(k == 1, 5, 2 * k + 2))
        high = jnp.where(k == 0, 5, 2 * k + 4)
        lax.fori_loop(low, high, one_item, 0)
        total = None
        for part in range(4):
            total = weigh(3, high - 1, 1, part * 256, 256, total)
        conclude(3, high - 1, weigh(3, high - 1, 1, 1024, 128, total))

        @pl.when(k == 0)
        def _():
            await_sends(me, send, arrived, send_sem, recv_sem)
            for i in range(1, 4):
                local[i].wait()
                remote[i].wait_recv()

        @pl.when(k < 2)
        def _():
            finish(k, 1)

        @pl.when(k >= 2)
        def _():
            finish(2 * k - 2, 2)

        return carry

    lax.fori_loop(0, GROUPS + 1, stretch, 0)

    def passing(half, group, recv):
        start = pl.multiple_of(half * HALF + group * GROUP, GROUP)
        return relay(me, back, start, GROUP, rsend_sem.at[group], recv.at[group])

    def hand_on(groups, awaited):
        for group in groups:
            passing(me.c, group, brecv_sem).wait_recv()
            passing(me.c, group, rrecv_sem).start()
        for group in awaited:
            passing(1 - me.c, group, rrecv_sem).wait_recv()

    def place_early(i, carry):
        start = pl.multiple_of(me.c * HALF + i * 256, 256)
        column = slot_column(local_slots(rank[:, pl.ds(start, 256)], me.s))
        total = None
        for base in group_bases(me.y):
            value = dot(picks(column, base), back[pl.ds(base, GROUP), :])
            total = value if total is None else total + value
        placed[pl.ds(start, 256), :] = total.astype(BF16)
        return carry

    def placed_half(half):
        start = pl.multiple_of(half * HALF, HALF)
        rows = pl.ds(start, HALF)
        return (
            relay(me, placed, start, HALF, psend_sem, precv_sem),
            pltpu.make_async_copy(placed.at[rows], part_ref.at[rows], out_sem.at[4 + half]),
        )

    hand_on([me.group(0), me.group(2)], [me.group(0), me.group(2)])
    lax.fori_loop(0, HALF // 256, place_early, 0)
    to_partner, own_out = placed_half(me.c)
    from_partner, partner_out = placed_half(1 - me.c)
    to_partner.start()
    own_out.start()
    def late_rows(half, j):
        group = me.group(j)
        src = back.at[pl.ds(pl.multiple_of(half * HALF + group * GROUP, GROUP), GROUP)]
        spot = half * 2 + lax.rem(group, 2)
        dst = late_ref.at[pl.ds(pl.multiple_of(spot * GROUP, GROUP), GROUP)]
        there = pltpu.make_async_remote_copy(
            src_ref=src,
            dst_ref=dst,
            send_sem=rsend_sem.at[group],
            recv_sem=rrecv_sem.at[group],
            device_id=me.partner,
            device_id_type=MESH,
        )
        return src, dst, there

    outs = [own_out, partner_out]
    for j in (3, 1):
        passing(me.c, me.group(j), brecv_sem).wait_recv()
        src, dst, there = late_rows(me.c, j)
        there.start()
        here = pltpu.make_async_copy(src, dst, out_sem.at[j // 2])
        here.start()
        outs.append(here)
        if j == 3:
            from_partner.wait_recv()
            partner_out.start()
    for j in (3, 1):
        late_rows(1 - me.c, j)[2].wait_recv()
    to_partner.wait_send()
    for group in range(GROUPS):
        passing(me.c, group, rrecv_sem).wait_send()
    for copy in outs:
        copy.wait()
    await_sends(me, send, back, bsend_sem, brecv_sem)
    for j in range(GROUPS):
        for copy in exchange(me.c, me.group(j)):
            copy.wait_send()
    for copy in remote:
        copy.wait_send()


def place_kernel(rank, part, late, out):
    me = Place()
    column = slot_column(local_slots(rank[...], me.s))
    total = part[...].astype(F32)
    for i, base in enumerate(group_bases(1 - me.y)):
        total = total + dot(picks(column, base), late[pl.ds(i * GROUP, GROUP), :])
    out[...] = total.astype(BF16)


def body(
    points, curve_rank, patch_counts, norm_gain_attn, w_qkv, w_out, norm_gain_mlp, w_fc1, w_fc2
):
    rank = curve_rank.reshape(1, LENGTH)
    shape = jax.ShapeDtypeStruct
    vm = pl.BlockSpec(memory_space=pltpu.VMEM)
    anywhere = pl.BlockSpec(memory_space=pl.ANY)
    dma = pltpu.SemaphoreType.DMA
    part, late = pl.pallas_call(
        layer_kernel,
        name="layer",
        out_shape=(shape((LENGTH, FEAT), BF16), shape((HALF, FEAT), BF16)),
        in_specs=[anywhere] * 9,
        out_specs=[anywhere] * 2,
        scratch_shapes=[
            VMEM((LENGTH, FEAT), BF16),
            VMEM((1, LENGTH), jnp.int32),
            pltpu.SMEM((1, 4), jnp.int32),
            VMEM((1, FEAT), F32),
            VMEM((1, FEAT), F32),
            VMEM((LENGTH, FEAT), BF16),
            VMEM((LENGTH, FEAT), BF16),
            VMEM((HALF, FEAT), BF16),
            VMEM((HALF, FEAT), BF16),
            VMEM((2,) + w_qkv.shape, BF16),
            VMEM((2,) + w_out.shape, BF16),
            VMEM((2,) + w_fc1.shape, BF16),
            VMEM((2,) + w_fc2.shape, BF16),
            VMEM((4, 16, 128, 128), BF16),
            VMEM((16, 128, 128), BF16),
            VMEM((4, 16, 144, 128), BF16),
            VMEM((8, 4, 256, 256), BF16),
            VMEM((ITEMS + 1, 128, FEAT), BF16),
            VMEM((WIN, 256), F32),
            VMEM((WIN, 256), F32),
            VMEM((WIN, 256), BF16),
            VMEM((WIN, 256), BF16),
            VMEM((8, 256), F32),
            VMEM((8, 256), F32),
            pltpu.SMEM((4, 16), jnp.int32),
            dma, dma((4,)), dma((4,)), dma((4,)), dma((4,)), dma((4,)), dma((4,)),
            dma((4,)), dma((4,)), dma, dma((4,)), dma((4,)), dma((4,)), dma((6,)), dma((5,)), dma, dma,
        ],
        compiler_params=pltpu.CompilerParams(collective_id=0, has_side_effects=True),
    )(
        points, rank, patch_counts, norm_gain_attn.reshape(1, FEAT), w_qkv, w_out,
        norm_gain_mlp.reshape(1, FEAT), w_fc1, w_fc2,
    )

    return pl.pallas_call(
        place_kernel,
        name="place_rows",
        grid=(LENGTH // 1024,),
        out_shape=shape((LENGTH, FEAT), BF16),
        in_specs=[
            pl.BlockSpec((1, 1024), lambda i: (0, i)),
            pl.BlockSpec((1024, FEAT), lambda i: (i, 0)),
            pl.BlockSpec((HALF, FEAT), lambda i: (0, 0)),
        ],
        out_specs=pl.BlockSpec((1024, FEAT), lambda i: (i, 0)),
    )(rank, part, late)


def solution(mesh):
    placed = (
        P("space", None),
        P("space"),
        P("space", None),
        P(),
        P(None, None, "mp"),
        P("mp", None),
        P(),
        P(None, "mp"),
        P("mp", None),
    )
    return jax.shard_map(
        body, mesh=mesh, in_specs=placed, out_specs=P("space", None), check_vma=False
    )
```

```python
import functools
import math

import jax
import jax.numpy as jnp
from jax import lax
from jax.experimental import pallas as pl
from jax.experimental.pallas import tpu as pltpu
from jax.sharding import PartitionSpec as P

HDIM = 64
EPS = 1e-06
FAR = -1e30
QSCALE = math.log2(math.e) / math.sqrt(HDIM)

LENGTH = 2048
FEAT = 512
HALF = 1024
SHARDS = 128
PEERS = 64
CELL = 16
GROUP = 256
GROUPS = 4
NX, NZ = 4, 8

MESH = pl.DeviceIdType.MESH
VMEM = pltpu.VMEM
F32 = jnp.float32
BF16 = jnp.bfloat16


def dot(a, b):
    return jnp.dot(a, b, preferred_element_type=F32)


def norm_rows(values, gain):
    average = jnp.mean(values, axis=-1, keepdims=True)
    centred = values - average
    second = jnp.mean(centred * centred, axis=-1, keepdims=True)
    return (centred * lax.rsqrt(second + EPS) * gain).astype(BF16)


def twice_gelu(x):
    scale = math.sqrt(2.0 / math.pi)
    inner = x * (scale + (scale * 0.044715) * (x * x))
    return (x * (1.0 + jnp.tanh(inner))).astype(BF16)


class Place:
    def __init__(self):
        self.s = lax.axis_index("space")
        self.c = lax.axis_index("mp")
        self.x = lax.rem(self.s, NX)
        self.z = lax.rem(self.s // NX, NZ)
        self.h = self.s // PEERS
        self.own = self.s - self.h * PEERS
        self.y = self.own // 32
        self.partner = (self.s, 1 - self.c)
        self.has_self = self.h == self.c

    def group(self, j):
        near = self.z // (NZ // 2)
        zh = jnp.where(j < 2, 1 - near, near)
        return lax.rem(self.y + j, 2) * 2 + zh

    def block(self, n):
        return self.group(n // 2) * 2 + n % 2

    def peers(self, first, count):
        rows = [lax.rem(self.z + i, count // NX) * NX + first for i in range(count // NX)]
        places = [lax.rem(self.x + i, NX) for i in range(NX)]
        return [rows[q // NX] + places[q % NX] for q in range(count)]


def greet(me):
    barrier = pltpu.get_barrier_semaphore()

    places = [lax.rem(me.x + i, NX) for i in (2, 1, 3, 0)]

    def one(i, carry):
        away = NZ // 2 + (i + 1) // 2 * (2 * lax.rem(i, 2) - 1)
        first = lax.rem(me.z + away, NZ) * NX
        for y in range(2):
            for place in places:
                peer = first + (y * NZ * NX + place)

                @pl.when(jnp.logical_not(me.has_self & (peer == me.own)))
                def _():
                    pl.semaphore_signal(
                        barrier,
                        inc=1,
                        device_id=(me.c * PEERS + peer, me.h),
                        device_id_type=MESH,
                    )

        return carry

    lax.fori_loop(0, NZ, one, 0)
    pl.semaphore_signal(barrier, inc=1, device_id=me.partner, device_id_type=MESH)
    return barrier


def await_greetings(me, barrier):
    pl.semaphore_wait(barrier, jnp.where(me.has_self, PEERS, PEERS + 1))


def send_cells(me, first, count, src, dst, at, send_sem, recv_sem):
    landing = pl.multiple_of(at * CELL, CELL)
    mine = me.own // 16

    for peer in me.peers(first, count):

        @pl.when(jnp.logical_not(me.has_self & (peer == me.own)))
        def _():
            pltpu.make_async_remote_copy(
                src_ref=src.at[pl.ds(pl.multiple_of(peer * CELL, CELL), CELL)],
                dst_ref=dst.at[pl.ds(landing, CELL)],
                send_sem=send_sem,
                recv_sem=recv_sem.at[mine],
                device_id=(me.c * PEERS + peer, me.h),
                device_id_type=MESH,
            ).start()

    @pl.when(me.has_self & (me.own >= first) & (me.own < first + count))
    def _():
        pltpu.make_async_copy(
            src.at[pl.ds(pl.multiple_of(me.own * CELL, CELL), CELL)],
            dst.at[pl.ds(landing, CELL)],
            recv_sem.at[mine],
        ).start()


def await_sends(me, src, dst, send_sem, recv_sem):
    def over(rows):
        pltpu.make_async_remote_copy(
            src_ref=src.at[pl.ds(0, rows)],
            dst_ref=dst.at[pl.ds(0, rows)],
            send_sem=send_sem,
            recv_sem=recv_sem.at[0],
            device_id=me.partner,
            device_id_type=MESH,
        ).wait_send()

    @pl.when(me.has_self)
    def _():
        over(HALF - CELL)

    @pl.when(jnp.logical_not(me.has_self))
    def _():
        over(HALF)


def relay(me, buf, start, rows, send_sem, recv_sem):
    part = buf.at[pl.ds(start, rows)]
    return pltpu.make_async_remote_copy(
        src_ref=part,
        dst_ref=part,
        send_sem=send_sem,
        recv_sem=recv_sem,
        device_id=me.partner,
        device_id_type=MESH,
    )


def local_slots(rank, s):
    return (rank // LENGTH) * CELL + (rank % LENGTH) - s * CELL


def group_bases(y):
    return [
        pl.multiple_of(half * HALF + (2 * y + k) * GROUP, GROUP)
        for half in range(2)
        for k in range(2)
    ]


def slot_column(slots):
    return jnp.concatenate(
        [
            jnp.broadcast_to(slots[:, p * 128 : (p + 1) * 128], (128, 128)).T
            for p in range(slots.shape[1] // 128)
        ],
        axis=0,
    )


def picks(column, base):
    lane = lax.broadcasted_iota(jnp.int32, column.shape, 1)
    return jnp.concatenate(
        [
            jnp.where(column == lane + (base + t * 128), 1.0, 0.0).astype(BF16)
            for t in range(GROUP // 128)
        ],
        axis=1,
    )


WIN = 1152
KEYS = 384
ITEMS = 11


def layer_kernel(
    points_in, rank_in, counts_in, gain_attn_in, w_qkv, w_out, gain_mlp_in, w_fc1, w_fc2,
    part_ref, late_ref, points, rank, counts, gain_attn, gain_mlp,
    back, placed, send, arrived, wq, wo, f1, f2, kk, marks, vt, qt, ctxv, s0, s1, p0, p1, m0, m1, table,
    send_sem, recv_sem, wloc_sem, wsend_sem, wrecv_sem, ksend_sem, krecv_sem,
    vsend_sem, vrecv_sem, bsend_sem, brecv_sem, rsend_sem, rrecv_sem,
    out_sem, load_sem, psend_sem, precv_sem,
):
    me = Place()
    loads = [
        pltpu.make_async_copy(src, dst, load_sem.at[i])
        for i, (src, dst) in enumerate(
            (
                (rank_in, rank),
                (points_in, points),
                (counts_in, counts),
                (gain_attn_in, gain_attn),
                (gain_mlp_in, gain_mlp),
            )
        )
    ]
    for copy in loads:
        copy.start()
    barrier = greet(me)
    loads[0].wait()
    slots = local_slots(rank[...], me.s)
    s_refs, p_refs, m_refs = (s0, s1), (p0, p1), (m0, m1)

    def permute(group):
        first = me.c * HALF + group * GROUP
        total = jnp.zeros((GROUP, FEAT), F32)
        for part in range(4):
            wanted = first + lax.broadcasted_iota(jnp.int32, (GROUP, 512), 0)
            hit = wanted == slots[:, part * 512 : (part + 1) * 512]
            pick = jnp.where(hit, 1.0, 0.0).astype(BF16)
            total = total + dot(pick, points[pl.ds(part * 512, 512), :])
        send[pl.ds(pl.multiple_of(group * GROUP, GROUP), GROUP), :] = total.astype(BF16)

    local, remote = [], []
    for i, (src, dst) in enumerate(((w_qkv, wq), (w_out, wo), (w_fc1, f1), (w_fc2, f2))):
        copy = pltpu.make_async_copy(src, dst.at[me.c], wloc_sem.at[i])
        copy.start()
        local.append(copy)
        remote.append(
            pltpu.make_async_remote_copy(
                src_ref=src,
                dst_ref=dst.at[me.c],
                send_sem=wsend_sem.at[i],
                recv_sem=wrecv_sem.at[i],
                device_id=me.partner,
                device_id_type=MESH,
            )
        )

    loads[1].wait()
    for j in range(GROUPS):
        group = me.group(j)
        permute(group)
        if j == 0:
            await_greetings(me, barrier)
            remote[0].start()
        send_cells(me, group * 16, 16, send, arrived, me.own, send_sem, recv_sem)
    for copy in remote[1:]:
        copy.start()

    for copy in loads[2:]:
        copy.wait()

    c1 = counts[0, 0]
    c2 = c1 + counts[0, 1]
    c3 = c2 + counts[0, 2]

    def patch_of(position):
        return (
            (position >= c1).astype(jnp.int32)
            + (position >= c2).astype(jnp.int32)
            + (position >= c3).astype(jnp.int32)
        )

    def mark_keys(i, carry):
        patch = patch_of(i * 128 + lax.broadcasted_iota(jnp.int32, (128, 128), 0))
        lane = lax.broadcasted_iota(jnp.int32, (128, 128), 1)
        marks[i] = jnp.where((lane < 4) & (lane != patch), FAR, 0.0).astype(BF16)
        for pair in range(4):
            vt[pair, i, 128:144, :] = jnp.ones((16, 128), BF16)
        return carry

    lax.fori_loop(0, LENGTH // 128, mark_keys, 0)

    def mark_queries(i, carry):
        first = me.c * HALF + i * 128
        patch = patch_of(first + lax.broadcasted_iota(jnp.int32, (128, 256), 1) % 128)
        row = lax.broadcasted_iota(jnp.int32, (128, 256), 0)
        mark = jnp.where(row == patch, 1.0, 0.0).astype(BF16)
        for pair in range(4):
            qt[i, pair, 128:256, :] = mark
        return carry

    lax.fori_loop(0, 8, mark_queries, 0)

    zero = c1 * 0
    firsts, lasts, begins, index = [], [], [], zero
    for n in range(8):
        row = me.c * HALF + me.block(n) * 128
        firsts.append(patch_of(row))
        lasts.append(patch_of(row + 127))
        begins.append(index)
        index = index + lasts[n] - firsts[n] + 1
        table[2, n] = begins[n]
        table[3, n] = firsts[n]
    for i in range(ITEMS + 1):
        block, patch = me.block(0), jnp.minimum(firsts[0] + i, lasts[0])
        for n in range(1, 8):
            reached = begins[n] <= i
            block = jnp.where(reached, me.block(n), block)
            patch = jnp.where(
                reached, jnp.minimum(firsts[n] + i - begins[n], lasts[n]), patch
            )
        start = jnp.where(
            patch >= 3, c3, jnp.where(patch >= 2, c2, jnp.where(patch >= 1, c1, zero))
        )
        table[0, i + 1] = block
        table[1, i + 1] = jnp.minimum(start // 128, (LENGTH - WIN) // 128)

    local[0].wait()
    remote[0].wait_recv()

    def project(group):
        rows = pl.ds(pl.multiple_of(group * GROUP, GROUP), GROUP)
        place = me.c * 8 + group * 2
        normed = norm_rows(arrived[rows, :].astype(F32), gain_attn[...])
        row = lax.broadcasted_iota(jnp.int32, (128, 128), 0)
        to_keys, to_values = exchange(me.c, group)
        for half in range(2):
            values = dot(normed, wq[half, 2])
            for p in range(2):
                pair, cols = 2 * half + p, slice(p * 128, (p + 1) * 128)
                for b in range(2):
                    vt[pair, place + b, 0:128, :] = values[b * 128 : (b + 1) * 128, cols].T.astype(
                        BF16
                    )
        for half in range(2):
            keys = dot(normed, wq[half, 1]).astype(BF16)
            for p in range(2):
                pair, cols = 2 * half + p, slice(p * 128, (p + 1) * 128)
                for b in range(2):
                    kk[pair, place + b] = keys[b * 128 : (b + 1) * 128, cols]
        to_values.start()
        for half in range(2):
            queries = dot(normed, wq[half, 0]) * QSCALE
            for p in range(2):
                pair, cols = 2 * half + p, slice(p * 128, (p + 1) * 128)
                for b in range(2):
                    turned = queries[b * 128 : (b + 1) * 128, cols].T
                    block = group * 2 + b
                    qt[block, pair, 0:128, 0:128] = jnp.where(row < HDIM, turned, 0.0).astype(BF16)
                    qt[block, pair, 0:128, 128:256] = jnp.where(row >= HDIM, turned, 0.0).astype(
                        BF16
                    )
            if half == 0:
                to_keys.start()

    def exchange(half, group):
        place = half * 8 + group * 2
        k_part = kk.at[:, pl.ds(place, 2)]
        v_part = vt.at[:, pl.ds(place, 2), pl.ds(0, 128)]
        return [
            pltpu.make_async_remote_copy(
                src_ref=part,
                dst_ref=part,
                send_sem=ss.at[group],
                recv_sem=rs.at[group],
                device_id=me.partner,
                device_id_type=MESH,
            )
            for part, ss, rs in (
                (k_part, ksend_sem, krecv_sem),
                (v_part, vsend_sem, vrecv_sem),
            )
        ]

    for j in (0, 2, 3, 1):
        group = me.group(j)
        relay(
            me, arrived, pl.multiple_of(group * GROUP, GROUP), GROUP,
            rsend_sem.at[group], recv_sem.at[group],
        ).wait_recv()
        project(group)
    for j in range(GROUPS):
        for copy in exchange(1 - me.c, me.group(j)):
            copy.wait_recv()

    def score(pair, item, part, dst, top):
        keys = pl.ds(table[1, item] + part * (KEYS // 128), KEYS // 128)
        lhs = jnp.concatenate([kk[pair, keys], marks[keys]], axis=2).reshape(KEYS, 256)
        value = dot(lhs, qt[table[0, item], pair])
        s_refs[dst][part * KEYS : (part + 1) * KEYS, :] = value
        high = jnp.max(value.reshape(KEYS // 8, 8, 256), axis=0)
        return high if top is None else jnp.maximum(top, high)

    def settle(dst, top):
        m_refs[dst][...] = jnp.broadcast_to(jnp.max(top, axis=0, keepdims=True), (8, 256))

    def raise_part(src, part, top):
        rows = slice(part * 128, (part + 1) * 128)
        p_refs[src][rows, :] = jnp.exp2(s_refs[src][rows, :] - top).astype(BF16)

    def weigh(pair, item, src, low, count, total):
        start = table[1, item] + low // 128
        lhs = [vt[pair, start + b] for b in range(count // 128)]
        lhs = jnp.concatenate(lhs, axis=1) if count > 128 else lhs[0]
        value = dot(lhs, p_refs[src][low : low + count, :])
        return value if total is None else total + value

    def conclude(pair, item, total):
        inverse = 1.0 / total[128:129, :]
        result = jnp.concatenate(
            [
                total[0:64, 0:128] * inverse[:, 0:128],
                total[64:128, 128:256] * inverse[:, 128:256],
            ],
            axis=0,
        )
        ctxv[item, :, pair * 128 : (pair + 1) * 128] = result.T.astype(BF16)

    def step(item, pair, settled=False):
        now, other = pair % 2, 1 - pair % 2
        after, after_pair = (item, pair + 1) if pair < 3 else (item + 1, 0)
        before, before_pair = (item, pair - 1) if pair > 0 else (item - 1, 3)
        top = m_refs[now][0:1, :]
        high = total = None
        for part in range(9):
            if part % 3 == 0:
                high = score(after_pair, after, part // 3, other, high)
            raise_part(now, part, top)
            if part % 2 == 1 and not settled:
                total = weigh(before_pair, before, other, (part - 1) * 128, 256, total)
        if not settled:
            total = weigh(before_pair, before, other, 1024, 128, total)
            conclude(before_pair, before, total)
        settle(other, high)

    def one_item(item, carry):
        for pair in range(4):
            step(item, pair)
        return carry

    high = None
    for part in range(3):
        high = score(0, 1, part, 0, high)
    settle(0, high)

    def block_context(n):
        begin, first = table[2, n] + 1, table[3, n]
        row = me.c * HALF + me.block(n) * 128
        place = lax.broadcasted_iota(jnp.int32, (128, FEAT), 0)
        value = ctxv[begin]
        for e in range(1, 4):
            patch = first + e
            start = jnp.where(
                patch == 1, c1, jnp.where(patch == 2, c2, jnp.where(patch == 3, c3, LENGTH))
            )
            other = ctxv[jnp.minimum(begin + e, ITEMS)]
            value = jnp.where(place >= start - row, other, value)
        return value

    def finish(n, blocks):
        ctx = [block_context(n + b) for b in range(blocks)]
        ctx = jnp.concatenate(ctx, axis=0) if blocks > 1 else ctx[0]
        block = me.block(n)
        rows = pl.ds(pl.multiple_of(block * 128, 128), blocks * 128)
        attn = dot(ctx[:, :256], wo[0]) + dot(ctx[:, 256:], wo[1])
        middle = (arrived[rows, :].astype(F32) + attn.astype(BF16).astype(F32)).astype(BF16)
        middle = middle.astype(F32)
        normed = norm_rows(middle, gain_mlp[...])
        total = None
        for half in range(2):
            value = dot(twice_gelu(dot(normed, f1[half])), f2[half])
            total = value if total is None else total + value
        send[rows, :] = (middle + 0.5 * total).astype(BF16)
        send_cells(me, block * 8, blocks * 8, send, back, me.s, bsend_sem, brecv_sem)

    def stretch(k, carry):
        low = jnp.where(k == 0, 1, jnp.where(k == 1, 5, 2 * k + 2))
        high = jnp.where(k == 0, 5, 2 * k + 4)
        for pair in range(4):
            step(low, pair, settled=pair == 0)
        lax.fori_loop(low + 1, high, one_item, 0)
        total = None
        for part in range(4):
            total = weigh(3, high - 1, 1, part * 256, 256, total)
        conclude(3, high - 1, weigh(3, high - 1, 1, 1024, 128, total))

        @pl.when(k == 0)
        def _():
            await_sends(me, send, arrived, send_sem, recv_sem)
            for i in range(1, 4):
                local[i].wait()
                remote[i].wait_recv()

        @pl.when(k < 2)
        def _():
            finish(k, 1)

        @pl.when(k >= 2)
        def _():
            finish(2 * k - 2, 2)

        return carry

    lax.fori_loop(0, GROUPS + 1, stretch, 0)

    def passing(half, group, recv):
        start = pl.multiple_of(half * HALF + group * GROUP, GROUP)
        return relay(me, back, start, GROUP, rsend_sem.at[group], recv.at[group])

    def hand_on(groups, awaited):
        for group in groups:
            passing(me.c, group, brecv_sem).wait_recv()
            passing(me.c, group, rrecv_sem).start()
        for group in awaited:
            passing(1 - me.c, group, rrecv_sem).wait_recv()

    def place_early(i, carry):
        start = pl.multiple_of(me.c * HALF + i * 256, 256)
        column = slot_column(local_slots(rank[:, pl.ds(start, 256)], me.s))
        total = None
        for base in group_bases(me.y):
            value = dot(picks(column, base), back[pl.ds(base, GROUP), :])
            total = value if total is None else total + value
        placed[pl.ds(start, 256), :] = total.astype(BF16)
        return carry

    def placed_half(half):
        start = pl.multiple_of(half * HALF, HALF)
        rows = pl.ds(start, HALF)
        return (
            relay(me, placed, start, HALF, psend_sem, precv_sem),
            pltpu.make_async_copy(placed.at[rows], part_ref.at[rows], out_sem.at[4 + half]),
        )

    hand_on([me.group(0), me.group(2)], [me.group(0), me.group(2)])
    lax.fori_loop(0, HALF // 256, place_early, 0)
    to_partner, own_out = placed_half(me.c)
    from_partner, partner_out = placed_half(1 - me.c)
    to_partner.start()
    own_out.start()
    def late_rows(half, j):
        group = me.group(j)
        src = back.at[pl.ds(pl.multiple_of(half * HALF + group * GROUP, GROUP), GROUP)]
        spot = half * 2 + lax.rem(group, 2)
        dst = late_ref.at[pl.ds(pl.multiple_of(spot * GROUP, GROUP), GROUP)]
        there = pltpu.make_async_remote_copy(
            src_ref=src,
            dst_ref=dst,
            send_sem=rsend_sem.at[group],
            recv_sem=rrecv_sem.at[group],
            device_id=me.partner,
            device_id_type=MESH,
        )
        return src, dst, there

    outs = [own_out, partner_out]
    for j in (3, 1):
        passing(me.c, me.group(j), brecv_sem).wait_recv()
        src, dst, there = late_rows(me.c, j)
        there.start()
        here = pltpu.make_async_copy(src, dst, out_sem.at[j // 2])
        here.start()
        outs.append(here)
        if j == 3:
            from_partner.wait_recv()
            partner_out.start()
    for j in (3, 1):
        late_rows(1 - me.c, j)[2].wait_recv()
    to_partner.wait_send()
    for group in range(GROUPS):
        passing(me.c, group, rrecv_sem).wait_send()
    for copy in outs:
        copy.wait()
    await_sends(me, send, back, bsend_sem, brecv_sem)
    for j in range(GROUPS):
        for copy in exchange(me.c, me.group(j)):
            copy.wait_send()
    for copy in remote:
        copy.wait_send()


def place_kernel(rank, part, late, out):
    me = Place()
    column = slot_column(local_slots(rank[...], me.s))
    total = part[...].astype(F32)
    for i, base in enumerate(group_bases(1 - me.y)):
        total = total + dot(picks(column, base), late[pl.ds(i * GROUP, GROUP), :])
    out[...] = total.astype(BF16)


def body(
    points, curve_rank, patch_counts, norm_gain_attn, w_qkv, w_out, norm_gain_mlp, w_fc1, w_fc2
):
    rank = curve_rank.reshape(1, LENGTH)
    shape = jax.ShapeDtypeStruct
    vm = pl.BlockSpec(memory_space=pltpu.VMEM)
    anywhere = pl.BlockSpec(memory_space=pl.ANY)
    dma = pltpu.SemaphoreType.DMA
    part, late = pl.pallas_call(
        layer_kernel,
        name="layer",
        out_shape=(shape((LENGTH, FEAT), BF16), shape((HALF, FEAT), BF16)),
        in_specs=[anywhere] * 9,
        out_specs=[anywhere] * 2,
        scratch_shapes=[
            VMEM((LENGTH, FEAT), BF16),
            VMEM((1, LENGTH), jnp.int32),
            pltpu.SMEM((1, 4), jnp.int32),
            VMEM((1, FEAT), F32),
            VMEM((1, FEAT), F32),
            VMEM((LENGTH, FEAT), BF16),
            VMEM((LENGTH, FEAT), BF16),
            VMEM((HALF, FEAT), BF16),
            VMEM((HALF, FEAT), BF16),
            VMEM((2,) + w_qkv.shape, BF16),
            VMEM((2,) + w_out.shape, BF16),
            VMEM((2,) + w_fc1.shape, BF16),
            VMEM((2,) + w_fc2.shape, BF16),
            VMEM((4, 16, 128, 128), BF16),
            VMEM((16, 128, 128), BF16),
            VMEM((4, 16, 144, 128), BF16),
            VMEM((8, 4, 256, 256), BF16),
            VMEM((ITEMS + 1, 128, FEAT), BF16),
            VMEM((WIN, 256), F32),
            VMEM((WIN, 256), F32),
            VMEM((WIN, 256), BF16),
            VMEM((WIN, 256), BF16),
            VMEM((8, 256), F32),
            VMEM((8, 256), F32),
            pltpu.SMEM((4, 16), jnp.int32),
            dma, dma((4,)), dma((4,)), dma((4,)), dma((4,)), dma((4,)), dma((4,)),
            dma((4,)), dma((4,)), dma, dma((4,)), dma((4,)), dma((4,)), dma((6,)), dma((5,)), dma, dma,
        ],
        compiler_params=pltpu.CompilerParams(collective_id=0, has_side_effects=True),
    )(
        points, rank, patch_counts, norm_gain_attn.reshape(1, FEAT), w_qkv, w_out,
        norm_gain_mlp.reshape(1, FEAT), w_fc1, w_fc2,
    )

    return pl.pallas_call(
        place_kernel,
        name="place_rows",
        grid=(LENGTH // 1024,),
        out_shape=shape((LENGTH, FEAT), BF16),
        in_specs=[
            pl.BlockSpec((1, 1024), lambda i: (0, i)),
            pl.BlockSpec((1024, FEAT), lambda i: (i, 0)),
            pl.BlockSpec((HALF, FEAT), lambda i: (0, 0)),
        ],
        out_specs=pl.BlockSpec((1024, FEAT), lambda i: (i, 0)),
    )(rank, part, late)


def solution(mesh):
    placed = (
        P("space", None),
        P("space"),
        P("space", None),
        P(),
        P(None, None, "mp"),
        P("mp", None),
        P(),
        P(None, "mp"),
        P("mp", None),
    )
    return jax.shard_map(
        body, mesh=mesh, in_specs=placed, out_specs=P("space", None), check_vma=False
    )
```

```python
import functools
import math

import jax
import jax.numpy as jnp
from jax import lax
from jax.experimental import pallas as pl
from jax.experimental.pallas import tpu as pltpu
from jax.sharding import PartitionSpec as P

HDIM = 64
EPS = 1e-06
FAR = -1e30
QSCALE = math.log2(math.e) / math.sqrt(HDIM)

LENGTH = 2048
FEAT = 512
HALF = 1024
SHARDS = 128
PEERS = 64
CELL = 16
GROUP = 256
GROUPS = 4
NX, NZ = 4, 8

MESH = pl.DeviceIdType.MESH
VMEM = pltpu.VMEM
F32 = jnp.float32
BF16 = jnp.bfloat16


def dot(a, b):
    return jnp.dot(a, b, preferred_element_type=F32)


def norm_rows(values, gain):
    average = jnp.mean(values, axis=-1, keepdims=True)
    centred = values - average
    second = jnp.mean(centred * centred, axis=-1, keepdims=True)
    return (centred * lax.rsqrt(second + EPS) * gain).astype(BF16)


def twice_gelu(x):
    scale = math.sqrt(2.0 / math.pi)
    inner = x * (scale + (scale * 0.044715) * (x * x))
    return (x * (1.0 + jnp.tanh(inner))).astype(BF16)


class Place:
    def __init__(self):
        self.s = lax.axis_index("space")
        self.c = lax.axis_index("mp")
        self.x = lax.rem(self.s, NX)
        self.z = lax.rem(self.s // NX, NZ)
        self.h = self.s // PEERS
        self.own = self.s - self.h * PEERS
        self.y = self.own // 32
        self.partner = (self.s, 1 - self.c)
        self.has_self = self.h == self.c

    def group(self, j):
        near = self.z // (NZ // 2)
        zh = jnp.where(j < 2, 1 - near, near)
        return lax.rem(self.y + j, 2) * 2 + zh

    def block(self, n):
        return self.group(n // 2) * 2 + n % 2

    def peers(self, first, count):
        rows = [lax.rem(self.z + i, count // NX) * NX + first for i in range(count // NX)]
        places = [lax.rem(self.x + i, NX) for i in range(NX)]
        return [rows[q // NX] + places[q % NX] for q in range(count)]


def greet(me):
    barrier = pltpu.get_barrier_semaphore()

    places = [lax.rem(me.x + i, NX) for i in (2, 1, 3, 0)]

    def one(i, carry):
        away = NZ // 2 + (i + 1) // 2 * (2 * lax.rem(i, 2) - 1)
        first = lax.rem(me.z + away, NZ) * NX
        for y in range(2):
            for place in places:
                peer = first + (y * NZ * NX + place)

                @pl.when(jnp.logical_not(me.has_self & (peer == me.own)))
                def _():
                    pl.semaphore_signal(
                        barrier,
                        inc=1,
                        device_id=(me.c * PEERS + peer, me.h),
                        device_id_type=MESH,
                    )

        return carry

    lax.fori_loop(0, NZ, one, 0)
    pl.semaphore_signal(barrier, inc=1, device_id=me.partner, device_id_type=MESH)
    return barrier


def await_greetings(me, barrier):
    pl.semaphore_wait(barrier, jnp.where(me.has_self, PEERS, PEERS + 1))


def send_cells(me, first, count, src, dst, at, send_sem, recv_sem):
    landing = pl.multiple_of(at * CELL, CELL)
    mine = me.own // 16

    for peer in me.peers(first, count):

        @pl.when(jnp.logical_not(me.has_self & (peer == me.own)))
        def _():
            pltpu.make_async_remote_copy(
                src_ref=src.at[pl.ds(pl.multiple_of(peer * CELL, CELL), CELL)],
                dst_ref=dst.at[pl.ds(landing, CELL)],
                send_sem=send_sem,
                recv_sem=recv_sem.at[mine],
                device_id=(me.c * PEERS + peer, me.h),
                device_id_type=MESH,
            ).start()

    @pl.when(me.has_self & (me.own >= first) & (me.own < first + count))
    def _():
        pltpu.make_async_copy(
            src.at[pl.ds(pl.multiple_of(me.own * CELL, CELL), CELL)],
            dst.at[pl.ds(landing, CELL)],
            recv_sem.at[mine],
        ).start()


def await_sends(me, src, dst, send_sem, recv_sem):
    def over(rows):
        pltpu.make_async_remote_copy(
            src_ref=src.at[pl.ds(0, rows)],
            dst_ref=dst.at[pl.ds(0, rows)],
            send_sem=send_sem,
            recv_sem=recv_sem.at[0],
            device_id=me.partner,
            device_id_type=MESH,
        ).wait_send()

    @pl.when(me.has_self)
    def _():
        over(HALF - CELL)

    @pl.when(jnp.logical_not(me.has_self))
    def _():
        over(HALF)


def relay(me, buf, start, rows, send_sem, recv_sem):
    part = buf.at[pl.ds(start, rows)]
    return pltpu.make_async_remote_copy(
        src_ref=part,
        dst_ref=part,
        send_sem=send_sem,
        recv_sem=recv_sem,
        device_id=me.partner,
        device_id_type=MESH,
    )


def local_slots(rank, s):
    return (rank // LENGTH) * CELL + (rank % LENGTH) - s * CELL


def group_bases(y):
    return [
        pl.multiple_of(half * HALF + (2 * y + k) * GROUP, GROUP)
        for half in range(2)
        for k in range(2)
    ]


def slot_column(slots):
    return jnp.concatenate(
        [
            jnp.broadcast_to(slots[:, p * 128 : (p + 1) * 128], (128, 128)).T
            for p in range(slots.shape[1] // 128)
        ],
        axis=0,
    )


def picks(column, base):
    lane = lax.broadcasted_iota(jnp.int32, column.shape, 1)
    return jnp.concatenate(
        [
            jnp.where(column == lane + (base + t * 128), 1.0, 0.0).astype(BF16)
            for t in range(GROUP // 128)
        ],
        axis=1,
    )


WIN = 1152
KEYS = 384
ITEMS = 11


def layer_kernel(
    points_in, rank_in, counts_in, gain_attn_in, w_qkv, w_out, gain_mlp_in, w_fc1, w_fc2,
    part_ref, late_ref, points, rank, counts, gain_attn, gain_mlp,
    back, placed, send, arrived, wq, wo, f1, f2, kk, marks, vt, qt, ctxv, s0, s1, p0, p1, m0, m1, table,
    send_sem, recv_sem, wloc_sem, wsend_sem, wrecv_sem, ksend_sem, krecv_sem,
    vsend_sem, vrecv_sem, bsend_sem, brecv_sem, rsend_sem, rrecv_sem,
    out_sem, load_sem, psend_sem, precv_sem,
):
    me = Place()
    loads = [
        pltpu.make_async_copy(src, dst, load_sem.at[i])
        for i, (src, dst) in enumerate(
            (
                (rank_in, rank),
                (points_in, points),
                (counts_in, counts),
                (gain_attn_in, gain_attn),
                (gain_mlp_in, gain_mlp),
            )
        )
    ]
    for copy in loads:
        copy.start()
    barrier = greet(me)
    loads[0].wait()
    slots = local_slots(rank[...], me.s)
    s_refs, p_refs, m_refs = (s0, s1), (p0, p1), (m0, m1)

    def permute(group):
        first = me.c * HALF + group * GROUP
        total = jnp.zeros((GROUP, FEAT), F32)
        for part in range(4):
            wanted = first + lax.broadcasted_iota(jnp.int32, (GROUP, 512), 0)
            hit = wanted == slots[:, part * 512 : (part + 1) * 512]
            pick = jnp.where(hit, 1.0, 0.0).astype(BF16)
            total = total + dot(pick, points[pl.ds(part * 512, 512), :])
        send[pl.ds(pl.multiple_of(group * GROUP, GROUP), GROUP), :] = total.astype(BF16)

    local, remote = [], []
    for i, (src, dst) in enumerate(((w_qkv, wq), (w_out, wo), (w_fc1, f1), (w_fc2, f2))):
        copy = pltpu.make_async_copy(src, dst.at[me.c], wloc_sem.at[i])
        copy.start()
        local.append(copy)
        remote.append(
            pltpu.make_async_remote_copy(
                src_ref=src,
                dst_ref=dst.at[me.c],
                send_sem=wsend_sem.at[i],
                recv_sem=wrecv_sem.at[i],
                device_id=me.partner,
                device_id_type=MESH,
            )
        )

    loads[1].wait()
    for j in range(GROUPS):
        group = me.group(j)
        permute(group)
        if j == 0:
            await_greetings(me, barrier)
            remote[0].start()
        send_cells(me, group * 16, 16, send, arrived, me.own, send_sem, recv_sem)
    for copy in remote[1:]:
        copy.start()

    for copy in loads[2:]:
        copy.wait()

    c1 = counts[0, 0]
    c2 = c1 + counts[0, 1]
    c3 = c2 + counts[0, 2]

    def patch_of(position):
        return (
            (position >= c1).astype(jnp.int32)
            + (position >= c2).astype(jnp.int32)
            + (position >= c3).astype(jnp.int32)
        )

    def mark_keys(i, carry):
        patch = patch_of(i * 128 + lax.broadcasted_iota(jnp.int32, (128, 128), 0))
        lane = lax.broadcasted_iota(jnp.int32, (128, 128), 1)
        marks[i] = jnp.where((lane < 4) & (lane != patch), FAR, 0.0).astype(BF16)
        for pair in range(4):
            vt[pair, i, 128:144, :] = jnp.ones((16, 128), BF16)
        return carry

    lax.fori_loop(0, LENGTH // 128, mark_keys, 0)

    def mark_queries(i, carry):
        first = me.c * HALF + i * 128
        patch = patch_of(first + lax.broadcasted_iota(jnp.int32, (128, 256), 1) % 128)
        row = lax.broadcasted_iota(jnp.int32, (128, 256), 0)
        mark = jnp.where(row == patch, 1.0, 0.0).astype(BF16)
        for pair in range(4):
            qt[i, pair, 128:256, :] = mark
        return carry

    lax.fori_loop(0, 8, mark_queries, 0)

    zero = c1 * 0
    firsts, lasts, begins, index = [], [], [], zero
    for n in range(8):
        row = me.c * HALF + me.block(n) * 128
        firsts.append(patch_of(row))
        lasts.append(patch_of(row + 127))
        begins.append(index)
        index = index + lasts[n] - firsts[n] + 1
        table[2, n] = begins[n]
        table[3, n] = firsts[n]
    for i in range(ITEMS + 1):
        block, patch = me.block(0), jnp.minimum(firsts[0] + i, lasts[0])
        for n in range(1, 8):
            reached = begins[n] <= i
            block = jnp.where(reached, me.block(n), block)
            patch = jnp.where(
                reached, jnp.minimum(firsts[n] + i - begins[n], lasts[n]), patch
            )
        start = jnp.where(
            patch >= 3, c3, jnp.where(patch >= 2, c2, jnp.where(patch >= 1, c1, zero))
        )
        table[0, i + 1] = block
        table[1, i + 1] = jnp.minimum(start // 128, (LENGTH - WIN) // 128)

    local[0].wait()
    remote[0].wait_recv()

    def project(group):
        rows = pl.ds(pl.multiple_of(group * GROUP, GROUP), GROUP)
        place = me.c * 8 + group * 2
        normed = norm_rows(arrived[rows, :].astype(F32), gain_attn[...])
        row = lax.broadcasted_iota(jnp.int32, (128, 128), 0)
        to_keys, to_values = exchange(me.c, group)
        for half in range(2):
            values = dot(normed, wq[half, 2])
            for p in range(2):
                pair, cols = 2 * half + p, slice(p * 128, (p + 1) * 128)
                for b in range(2):
                    vt[pair, place + b, 0:128, :] = values[b * 128 : (b + 1) * 128, cols].T.astype(
                        BF16
                    )
        for half in range(2):
            keys = dot(normed, wq[half, 1]).astype(BF16)
            for p in range(2):
                pair, cols = 2 * half + p, slice(p * 128, (p + 1) * 128)
                for b in range(2):
                    kk[pair, place + b] = keys[b * 128 : (b + 1) * 128, cols]
        to_values.start()
        for half in range(2):
            queries = dot(normed, wq[half, 0]) * QSCALE
            for p in range(2):
                pair, cols = 2 * half + p, slice(p * 128, (p + 1) * 128)
                for b in range(2):
                    turned = queries[b * 128 : (b + 1) * 128, cols].T
                    block = group * 2 + b
                    qt[block, pair, 0:128, 0:128] = jnp.where(row < HDIM, turned, 0.0).astype(BF16)
                    qt[block, pair, 0:128, 128:256] = jnp.where(row >= HDIM, turned, 0.0).astype(
                        BF16
                    )
            if half == 0:
                to_keys.start()

    def exchange(half, group):
        place = half * 8 + group * 2
        k_part = kk.at[:, pl.ds(place, 2)]
        v_part = vt.at[:, pl.ds(place, 2), pl.ds(0, 128)]
        return [
            pltpu.make_async_remote_copy(
                src_ref=part,
                dst_ref=part,
                send_sem=ss.at[group],
                recv_sem=rs.at[group],
                device_id=me.partner,
                device_id_type=MESH,
            )
            for part, ss, rs in (
                (k_part, ksend_sem, krecv_sem),
                (v_part, vsend_sem, vrecv_sem),
            )
        ]

    for j in (0, 2, 3, 1):
        group = me.group(j)
        relay(
            me, arrived, pl.multiple_of(group * GROUP, GROUP), GROUP,
            rsend_sem.at[group], recv_sem.at[group],
        ).wait_recv()
        project(group)
    for j in range(GROUPS):
        for copy in exchange(1 - me.c, me.group(j)):
            copy.wait_recv()

    def score(pair, item, part, dst, top):
        keys = pl.ds(table[1, item] + part * (KEYS // 128), KEYS // 128)
        lhs = jnp.concatenate([kk[pair, keys], marks[keys]], axis=2).reshape(KEYS, 256)
        value = dot(lhs, qt[table[0, item], pair])
        s_refs[dst][part * KEYS : (part + 1) * KEYS, :] = value
        high = jnp.max(value.reshape(KEYS // 8, 8, 256), axis=0)
        return high if top is None else jnp.maximum(top, high)

    def settle(dst, top):
        m_refs[dst][...] = jnp.broadcast_to(jnp.max(top, axis=0, keepdims=True), (8, 256))

    def raise_part(src, part, top):
        rows = slice(part * 128, (part + 1) * 128)
        p_refs[src][rows, :] = jnp.exp2(s_refs[src][rows, :] - top).astype(BF16)

    def weigh(pair, item, src, low, count, total):
        start = table[1, item] + low // 128
        lhs = [vt[pair, start + b] for b in range(count // 128)]
        lhs = jnp.concatenate(lhs, axis=1) if count > 128 else lhs[0]
        value = dot(lhs, p_refs[src][low : low + count, :])
        return value if total is None else total + value

    def conclude(pair, item, total):
        inverse = 1.0 / total[128:129, :]
        result = jnp.concatenate(
            [
                total[0:64, 0:128] * inverse[:, 0:128],
                total[64:128, 128:256] * inverse[:, 128:256],
            ],
            axis=0,
        )
        ctxv[item, :, pair * 128 : (pair + 1) * 128] = result.T.astype(BF16)

    def step(item, pair):
        now, other = pair % 2, 1 - pair % 2
        after, after_pair = (item, pair + 1) if pair < 3 else (item + 1, 0)
        before, before_pair = (item, pair - 1) if pair > 0 else (item - 1, 3)
        top = m_refs[now][0:1, :]
        high = total = None
        for part in range(9):
            if part % 3 == 0:
                high = score(after_pair, after, part // 3, other, high)
            raise_part(now, part, top)
            if part % 2 == 1:
                total = weigh(before_pair, before, other, (part - 1) * 128, 256, total)
        total = weigh(before_pair, before, other, 1024, 128, total)
        conclude(before_pair, before, total)
        settle(other, high)

    def one_item(item, carry):
        for pair in range(4):
            step(item, pair)
        return carry

    table[0, 0] = table[0, 1]
    table[1, 0] = table[1, 1]
    p1[...] = jnp.zeros_like(p1)
    high = None
    for part in range(3):
        high = score(0, 1, part, 0, high)
    settle(0, high)

    def block_context(n):
        begin, first = table[2, n] + 1, table[3, n]
        row = me.c * HALF + me.block(n) * 128
        place = lax.broadcasted_iota(jnp.int32, (128, FEAT), 0)
        value = ctxv[begin]
        for e in range(1, 4):
            patch = first + e
            start = jnp.where(
                patch == 1, c1, jnp.where(patch == 2, c2, jnp.where(patch == 3, c3, LENGTH))
            )
            other = ctxv[jnp.minimum(begin + e, ITEMS)]
            value = jnp.where(place >= start - row, other, value)
        return value

    def finish(n, blocks):
        ctx = [block_context(n + b) for b in range(blocks)]
        ctx = jnp.concatenate(ctx, axis=0) if blocks > 1 else ctx[0]
        block = me.block(n)
        rows = pl.ds(pl.multiple_of(block * 128, 128), blocks * 128)
        attn = dot(ctx[:, :256], wo[0]) + dot(ctx[:, 256:], wo[1])
        middle = (arrived[rows, :].astype(F32) + attn.astype(BF16).astype(F32)).astype(BF16)
        middle = middle.astype(F32)
        normed = norm_rows(middle, gain_mlp[...])
        total = None
        for half in range(2):
            value = dot(twice_gelu(dot(normed, f1[half])), f2[half])
            total = value if total is None else total + value
        send[rows, :] = (middle + 0.5 * total).astype(BF16)
        send_cells(me, block * 8, blocks * 8, send, back, me.s, bsend_sem, brecv_sem)

    def stretch(k, carry):
        low = jnp.where(k == 0, 1, jnp.where(k == 1, 5, 2 * k + 2))
        high = jnp.where(k == 0, 5, 2 * k + 4)
        lax.fori_loop(low, high, one_item, 0)
        total = None
        for part in range(4):
            total = weigh(3, high - 1, 1, part * 256, 256, total)
        conclude(3, high - 1, weigh(3, high - 1, 1, 1024, 128, total))

        @pl.when(k == 0)
        def _():
            await_sends(me, send, arrived, send_sem, recv_sem)
            for i in range(1, 4):
                local[i].wait()
                remote[i].wait_recv()

        @pl.when(k < 2)
        def _():
            finish(k, 1)

        @pl.when(k >= 2)
        def _():
            finish(2 * k - 2, 2)

        return carry

    lax.fori_loop(0, GROUPS + 1, stretch, 0)

    def passing(half, group, recv):
        start = pl.multiple_of(half * HALF + group * GROUP, GROUP)
        return relay(me, back, start, GROUP, rsend_sem.at[group], recv.at[group])

    def hand_on(groups, awaited):
        for group in groups:
            passing(me.c, group, brecv_sem).wait_recv()
            passing(me.c, group, rrecv_sem).start()
        for group in awaited:
            passing(1 - me.c, group, rrecv_sem).wait_recv()

    def place_early(i, carry):
        start = pl.multiple_of(me.c * HALF + i * 256, 256)
        column = slot_column(local_slots(rank[:, pl.ds(start, 256)], me.s))
        total = None
        for base in group_bases(me.y):
            value = dot(picks(column, base), back[pl.ds(base, GROUP), :])
            total = value if total is None else total + value
        placed[pl.ds(start, 256), :] = total.astype(BF16)
        return carry

    def placed_half(half):
        start = pl.multiple_of(half * HALF, HALF)
        rows = pl.ds(start, HALF)
        return (
            relay(me, placed, start, HALF, psend_sem, precv_sem),
            pltpu.make_async_copy(placed.at[rows], part_ref.at[rows], out_sem.at[4 + half]),
        )

    hand_on([me.group(0), me.group(2)], [me.group(0), me.group(2)])
    lax.fori_loop(0, HALF // 256, place_early, 0)
    to_partner, own_out = placed_half(me.c)
    from_partner, partner_out = placed_half(1 - me.c)
    to_partner.start()
    own_out.start()
    def late_rows(half, j):
        group = me.group(j)
        src = back.at[pl.ds(pl.multiple_of(half * HALF + group * GROUP, GROUP), GROUP)]
        spot = half * 2 + lax.rem(group, 2)
        dst = late_ref.at[pl.ds(pl.multiple_of(spot * GROUP, GROUP), GROUP)]
        there = pltpu.make_async_remote_copy(
            src_ref=src,
            dst_ref=dst,
            send_sem=rsend_sem.at[group],
            recv_sem=rrecv_sem.at[group],
            device_id=me.partner,
            device_id_type=MESH,
        )
        return src, dst, there

    outs = [own_out, partner_out]
    for j in (3, 1):
        passing(me.c, me.group(j), brecv_sem).wait_recv()
        src, dst, there = late_rows(me.c, j)
        there.start()
        here = pltpu.make_async_copy(src, dst, out_sem.at[j // 2])
        here.start()
        outs.append(here)
        if j == 3:
            from_partner.wait_recv()
            partner_out.start()
    for j in (3, 1):
        late_rows(1 - me.c, j)[2].wait_recv()
    to_partner.wait_send()
    for group in range(GROUPS):
        passing(me.c, group, rrecv_sem).wait_send()
    for copy in outs:
        copy.wait()
    await_sends(me, send, back, bsend_sem, brecv_sem)
    for j in range(GROUPS):
        for copy in exchange(me.c, me.group(j)):
            copy.wait_send()
    for copy in remote:
        copy.wait_send()


def place_kernel(rank, part, late, out):
    me = Place()
    column = slot_column(local_slots(rank[...], me.s))
    total = part[...].astype(F32)
    for i, base in enumerate(group_bases(1 - me.y)):
        total = total + dot(picks(column, base), late[pl.ds(i * GROUP, GROUP), :])
    out[...] = total.astype(BF16)


def body(
    points, curve_rank, patch_counts, norm_gain_attn, w_qkv, w_out, norm_gain_mlp, w_fc1, w_fc2
):
    rank = curve_rank.reshape(1, LENGTH)
    shape = jax.ShapeDtypeStruct
    vm = pl.BlockSpec(memory_space=pltpu.VMEM)
    anywhere = pl.BlockSpec(memory_space=pl.ANY)
    dma = pltpu.SemaphoreType.DMA
    part, late = pl.pallas_call(
        layer_kernel,
        name="layer",
        out_shape=(shape((LENGTH, FEAT), BF16), shape((HALF, FEAT), BF16)),
        in_specs=[anywhere] * 9,
        out_specs=[anywhere] * 2,
        scratch_shapes=[
            VMEM((LENGTH, FEAT), BF16),
            VMEM((1, LENGTH), jnp.int32),
            pltpu.SMEM((1, 4), jnp.int32),
            VMEM((1, FEAT), F32),
            VMEM((1, FEAT), F32),
            VMEM((LENGTH, FEAT), BF16),
            VMEM((LENGTH, FEAT), BF16),
            VMEM((HALF, FEAT), BF16),
            VMEM((HALF, FEAT), BF16),
            VMEM((2,) + w_qkv.shape, BF16),
            VMEM((2,) + w_out.shape, BF16),
            VMEM((2,) + w_fc1.shape, BF16),
            VMEM((2,) + w_fc2.shape, BF16),
            VMEM((4, 16, 128, 128), BF16),
            VMEM((16, 128, 128), BF16),
            VMEM((4, 16, 144, 128), BF16),
            VMEM((8, 4, 256, 256), BF16),
            VMEM((ITEMS + 1, 128, FEAT), BF16),
            VMEM((WIN, 256), F32),
            VMEM((WIN, 256), F32),
            VMEM((WIN, 256), BF16),
            VMEM((WIN, 256), BF16),
            VMEM((8, 256), F32),
            VMEM((8, 256), F32),
            pltpu.SMEM((4, 16), jnp.int32),
            dma, dma((4,)), dma((4,)), dma((4,)), dma((4,)), dma((4,)), dma((4,)),
            dma((4,)), dma((4,)), dma, dma((4,)), dma((4,)), dma((4,)), dma((6,)), dma((5,)), dma, dma,
        ],
        compiler_params=pltpu.CompilerParams(collective_id=0, has_side_effects=True),
    )(
        points, rank, patch_counts, norm_gain_attn.reshape(1, FEAT), w_qkv, w_out,
        norm_gain_mlp.reshape(1, FEAT), w_fc1, w_fc2,
    )

    return pl.pallas_call(
        place_kernel,
        name="place_rows",
        grid=(LENGTH // 1024,),
        out_shape=shape((LENGTH, FEAT), BF16),
        in_specs=[
            pl.BlockSpec((1, 1024), lambda i: (0, i)),
            pl.BlockSpec((1024, FEAT), lambda i: (i, 0)),
            pl.BlockSpec((HALF, FEAT), lambda i: (0, 0)),
        ],
        out_specs=pl.BlockSpec((1024, FEAT), lambda i: (i, 0)),
    )(rank, part, late)


def solution(mesh):
    placed = (
        P("space", None),
        P("space"),
        P("space", None),
        P(),
        P(None, None, "mp"),
        P("mp", None),
        P(),
        P(None, "mp"),
        P("mp", None),
    )
    return jax.shard_map(
        body, mesh=mesh, in_specs=placed, out_specs=P("space", None), check_vma=False
    )
```
